32 devices in a mesh: tile: 16 (over z, x, core), group: 2 (over y).
Axes of the slice: x: 2, y: 2, z: 4, core: 2. Of those that a mesh axis runs over, the one named last changes fastest.
Arguments:
- object_field: float32 [2, 320, 2048], P(None, 'group', 'tile'), may hold values from -6 to 6
- probe_field: float32 [2, 256, 256], replicated, may hold values from -6 to 6
- amplitudes: float32 [32, 256, 256], P(('tile', 'group')), may hold values from 0 to 4
- row_start: int32 [32], P(('tile', 'group')), may hold values from 0 to 64
- column_start: int32 [32], P(('tile', 'group')), may hold values from 0 to 128
- live_slots: int32 [32], P(('tile', 'group')), may hold values 0 or 1
Outputs:
- new_object: float32 [2, 320, 2048], P(None, 'group', 'tile')
- new_probe: float32 [2, 256, 256], replicated
The draws below stay inside these ranges and needn't reach their ends.
All inputs are finite; a program needn't handle non-finite values. No bound on the sum of `live_slots` on one device may be relied on, other than what follows from the above.
Results may differ from the reference program's by a relative error of at most 0.0001.
Values sent between devices are 32-bit elements; how exact they have to be, the bound alone decides.
A program may use at most 64 MiB of HBM per device.

```python
import math
import jax
import jax.numpy as jnp
from jax import lax

WIN = 256
HALO = 128
ITERS = 1
OBJ_ROWS = 320
COLS_DEV = 128
POS_DEV = 1
OBJ_COLS = 2048
POSITIONS = 32
N_TILE = 16
N_GROUP = 2


def with_ends(drawn, own_key, smallest, top_value):
    longest = drawn.shape.index(max(drawn.shape))
    spots = []
    for shift in (0, 1):
        where = [jax.random.randint(jax.random.fold_in(own_key, axis), (), 0, length) for axis, length in enumerate(drawn.shape)]
        where[longest] = (where[longest] + shift) % drawn.shape[longest]
        spots.append(tuple(where))
    return drawn.at[spots[0]].set(smallest).at[spots[1]].set(top_value)


def shard_levels(stream_key, extent, split, least, top_value):
    def one(position, shards_of):
        steps = jax.random.uniform(jax.random.fold_in(jax.random.fold_in(stream_key, 6), position), (shards_of,), jnp.float32, least / len(split), top_value / len(split))
        return jnp.repeat(jnp.exp(steps), extent[position] // shards_of).reshape((-1,) + (1,) * (len(extent) - position - 1))

    gain = one(*split[0])
    for cut in split[1:]:
        gain = gain * one(*cut)
    return gain


def normal_values(key, dims, spread, most, pieces=(), held_as=jnp.bfloat16):
    drawn = jax.random.normal(key, dims, jnp.float32) * spread
    if len(pieces) > 0:
        drawn = shard_levels(key, dims, pieces, -0.22, 0.18) * drawn
    return jnp.clip(drawn, min=-most, max=most).astype(held_as)


def setup_inputs(seed: int = 0) -> dict:
    arg_keys = jax.random.split(jax.random.key(seed), 7)
    object_field = normal_values(arg_keys[0], (2, OBJ_ROWS, OBJ_COLS), 1.0, 6.0, ((1, 2), (2, 16)), jnp.float32)
    probe_field = normal_values(arg_keys[1], (2, WIN, WIN), 1.0, 6.0, (), jnp.float32)
    amplitudes = jnp.clip(4.0 * jax.random.uniform(arg_keys[2], (POSITIONS, WIN, WIN), jnp.float32) ** shard_levels(arg_keys[2], (POSITIONS, WIN, WIN), ((0, 32),), -0.2, 0.2), 0.0, 4.0)
    row_start = with_ends(jax.random.randint(arg_keys[3], (POSITIONS,), 0, OBJ_ROWS - WIN + 1), jax.random.fold_in(arg_keys[3], 1), 0, OBJ_ROWS - WIN).astype(jnp.int32)
    column_start = with_ends(jax.random.randint(arg_keys[4], (POSITIONS,), 0, COLS_DEV + 2 * HALO - WIN + 1), jax.random.fold_in(arg_keys[4], 1), 0, COLS_DEV + 2 * HALO - WIN).astype(jnp.int32)
    live_slots = with_ends((jax.random.randint(arg_keys[5], (POSITIONS,), 0, 4) < 3).astype(jnp.int32), jax.random.fold_in(arg_keys[5], 1), 0, 1)
    return dict(object_field=object_field, probe_field=probe_field, amplitudes=amplitudes, row_start=row_start, column_start=column_start, live_slots=live_slots)


def dft_tables(length):
    counter = jnp.arange(length, dtype=jnp.int32)
    product = counter[:, None] * counter[None, :] % length
    angles = 2.0 * math.pi / length * product.astype(jnp.float32)
    factor = 1.0 / math.sqrt(length)
    return (jnp.cos(angles) * factor, jnp.sin(angles) * factor)

def apply_left(matrix, values):
    return jnp.einsum('jk,pkl->pjl', matrix, values, precision=lax.Precision.HIGHEST)

def apply_right(values, matrix):
    return jnp.einsum('pjk,kl->pjl', values, matrix, precision=lax.Precision.HIGHEST)

def transform(real_part, imag_part, cos_table, sin_table, sign):
    left_real = apply_left(cos_table, real_part) - sign * apply_left(sin_table, imag_part)
    left_imag = apply_left(cos_table, imag_part) + sign * apply_left(sin_table, real_part)
    right_real = apply_right(left_real, cos_table) - sign * apply_right(left_imag, sin_table)
    right_imag = apply_right(left_imag, cos_table) + sign * apply_right(left_real, sin_table)
    return (right_real, right_imag)

def window_terms(windows, probe_field, amplitudes, live_slots, cos_table, sin_table):
    sample_real = windows[:, 0]
    sample_imag = windows[:, 1]
    probe_real = probe_field[0]
    probe_imag = probe_field[1]
    exit_real = probe_real * sample_real - probe_imag * sample_imag
    exit_imag = probe_real * sample_imag + probe_imag * sample_real
    far_real, far_imag = transform(exit_real, exit_imag, cos_table, sin_table, -1.0)
    modulus = jnp.maximum(jnp.sqrt(far_real * far_real + far_imag * far_imag), 0.25)
    factor = 1.0 - amplitudes / modulus
    miss_real, miss_imag = transform(far_real * factor, far_imag * factor, cos_table, sin_table, 1.0)
    weight = live_slots.astype(jnp.float32)[:, None, None]
    miss_real = miss_real * weight
    miss_imag = miss_imag * weight
    grad_real = probe_real * miss_real + probe_imag * miss_imag
    grad_imag = probe_real * miss_imag - probe_imag * miss_real
    probe_light = weight * (probe_real * probe_real + probe_imag * probe_imag)
    terms = jnp.stack([grad_real, grad_imag, probe_light], axis=1)
    probe_grad = jnp.stack([lax.optimization_barrier(jnp.sum(sample_real * miss_real + sample_imag * miss_imag, axis=0)), lax.optimization_barrier(jnp.sum(sample_real * miss_imag - sample_imag * miss_real, axis=0))], axis=0)
    window_light = lax.optimization_barrier(jnp.sum(weight * (sample_real * sample_real + sample_imag * sample_imag), axis=0))
    return (terms, probe_grad, window_light)

def add_windows(accum, terms, top_rows, left_edges):
    zero_index = jnp.zeros((), jnp.int32)

    def place(slot, current):
        corner = (zero_index, top_rows[slot], left_edges[slot])
        piece = lax.dynamic_slice(current, corner, (3, WIN, WIN))
        return lax.dynamic_update_slice(current, piece + terms[slot], corner)
    return lax.fori_loop(0, terms.shape[0], place, accum)

def cut_windows(padded, top_rows, left_edges):
    zero_index = jnp.zeros((), jnp.int32)

    def single(top_row, left_edge):
        return lax.dynamic_slice(padded, (zero_index, top_row, left_edge), (2, WIN, WIN))
    return jax.vmap(single)(top_rows, left_edges)

def apply_updates(object_field, probe_field, share, probe_grad, window_light):
    light_max = jnp.max(probe_field[0] * probe_field[0] + probe_field[1] * probe_field[1]) + 1e-06
    new_object = object_field - share[0:2] / (share[2:3] + 0.25 * light_max)
    new_probe = probe_field - probe_grad / (window_light + 0.25 * jnp.mean(window_light) + 1e-05)[None]
    return (new_object, new_probe)

def reference(object_field, probe_field, amplitudes, row_start, column_start, live_slots):
    cos_table, sin_table = dft_tables(WIN)
    blocks = N_TILE * N_GROUP
    tile_first = jnp.arange(blocks, dtype=jnp.int32) // N_GROUP * COLS_DEV
    block_cols = (column_start.reshape(blocks, POS_DEV).astype(jnp.int32) + tile_first[:, None]).astype(jnp.int32)
    block_rows = row_start.reshape(blocks, POS_DEV).astype(jnp.int32)
    block_amps = amplitudes.reshape(blocks, POS_DEV, WIN, WIN)
    block_live = live_slots.reshape(blocks, POS_DEV)
    for iteration in range(ITERS):
        padded = jnp.pad(object_field, ((0, 0), (0, 0), (HALO, HALO)))

        def visit(carry, block):
            grad_acc, probe_acc, light_acc = carry
            top_rows, left_edges, amps_here, live_here = block
            windows = cut_windows(padded, top_rows, left_edges)
            terms, probe_grad, window_light = window_terms(windows, probe_field, amps_here, live_here, cos_table, sin_table)
            grad_acc = add_windows(grad_acc, terms, top_rows, left_edges)
            return ((grad_acc, probe_acc + probe_grad, light_acc + window_light), None)
        start = (jnp.zeros((3, OBJ_ROWS, OBJ_COLS + 2 * HALO), jnp.float32), jnp.zeros((2, WIN, WIN), jnp.float32), jnp.zeros((WIN, WIN), jnp.float32))
        (grad_acc, probe_grad, window_light), unused = lax.scan(visit, start, (block_rows, block_cols, block_amps, block_live))
        share = grad_acc[:, :, HALO:HALO + OBJ_COLS]
        object_field, probe_field = apply_updates(object_field, probe_field, share, probe_grad, window_light)
    return (object_field, probe_field)
```

```python
import functools
import math

import jax
import jax.numpy as jnp
import numpy as np
from jax import lax
from jax.experimental import pallas as pl
from jax.experimental.pallas import tpu as pltpu
from jax.sharding import PartitionSpec as P

MESH = pl.DeviceIdType.MESH
F32 = jnp.float32
BF16 = jnp.bfloat16


def dft_tables(length):
    k = np.arange(length // 2)
    even = (2 * np.outer(k, k)) % length
    odd = np.outer(2 * k + 1, k) % length
    tables = []
    for turns in (even, odd):
        angles = 2.0 * math.pi / length * turns
        cos, sin = np.cos(angles) / math.sqrt(length), np.sin(angles) / math.sqrt(length)
        full = np.block([[cos, sin], [-sin, cos]])
        tables += [full, full.T]
    full = np.stack(tables).astype(np.float32)
    head = full.astype(BF16)
    tail = (full - head.astype(np.float32)).astype(BF16)
    return np.stack([head, tail], axis=1)


EVEN, EVEN_T, ODD, ODD_T = range(4)


def split(x):
    head = x.astype(BF16)
    return head, (x - head.astype(F32)).astype(BF16)


def mm(a, b):
    return jnp.dot(a, b, preferred_element_type=F32)


def cat(parts, axis):
    return jnp.concatenate(parts, axis=axis)


def table_left(table, x):
    head, tail = split(x)
    return mm(cat([table[0], table[0], table[1]], 1), cat([head, tail, head], 0))


def table_right(x, table):
    head, tail = split(x)
    return mm(cat([head, tail, head], 1), cat([table[0], table[0], table[1]], 0))


def fold_in(xr, xi, tables):
    n = xr.shape[0] // 2
    a = cat([xr[:n] + xr[n:], xi[:n] + xi[n:]], 0)
    b = cat([xr[:n] - xr[n:], xi[:n] - xi[n:]], 0)
    halves = table_left(tables[EVEN], a), table_left(tables[ODD], b)

    def sides(sign):
        rows = []
        for y in halves:
            yr, yi = y[:n], y[n:]
            rows.append(cat([yr[:, :n] + sign * yr[:, n:], yi[:, :n] + sign * yi[:, n:]], 1))
        return cat(rows, 0)

    return table_right(sides(1), tables[EVEN_T]), table_right(sides(-1), tables[ODD_T])


def fold_out(even, odd, tables):
    n = even.shape[0] // 2
    e, o = table_right(even, tables[EVEN]), table_right(odd, tables[ODD])
    plus, minus = e + o, e - o
    halves = []
    for q, table in ((0, tables[EVEN_T]), (1, tables[ODD_T])):
        r = slice(q * n, (q + 1) * n)
        halves.append(table_left(table, cat(
            [cat([plus[r, :n], minus[r, :n]], 1), cat([plus[r, n:], minus[r, n:]], 1)], 0)))
    plus, minus = halves[0] + halves[1], halves[0] - halves[1]
    return cat([plus[:n], minus[:n]], 0), cat([plus[n:], minus[n:]], 0)


def remote(src, dst, send, recv, tile, group):
    return pltpu.make_async_remote_copy(
        src_ref=src, dst_ref=dst, send_sem=send, recv_sem=recv,
        device_id={"tile": tile, "group": group}, device_id_type=MESH,
    )


class Plan:
    def __init__(self, T, G, W):
        self.H = T // 2
        self.owners = self.H // 2 if self.H % 4 == 0 else self.H
        self.first = (self.H - self.owners) // 2
        self.gs = max(n for n in range(1, G + 1) if G % n == 0 and n * self.owners * 8 <= W // 2)
        self.W, self.half = W, W // 2
        self.part = self.half // self.gs
        self.chunk = self.part // self.owners

    def here(self, t, g):
        self.t, self.g = t, g
        self.k, self.h = lax.div(t, 2), lax.rem(t, 2)
        self.partner = t + 1 - 2 * self.h
        self.s = lax.rem(g, self.gs)
        self.mine = self.k - self.first
        self.low = self.k < self.H // 2
        self.owner = jnp.logical_and(self.mine >= 0, self.mine < self.owners)

    def rows(self, h, s):
        return pl.ds(pl.multiple_of(h * self.half + s * self.part, 8), self.part)

    def chunk_rows(self, h, s, j):
        return pl.ds(pl.multiple_of(h * self.half + s * self.part + j * self.chunk, 8), self.chunk)

    def far_owner(self, i):
        return lax.rem(i + jnp.where(self.low, self.owners // 2, 0), self.owners)

    def near_owner(self, i):
        return jnp.where(self.low, i, self.owners - 1 - i)

    def far_chip(self, i):
        return jnp.where(self.low, self.H - 1 - i, i)


class Reduce:
    def __init__(self, plan, mine, came, send, recv):
        self.p, self.mine, self.came, self.send, self.recv = plan, mine, came, send, recv

    def copy(self, j):
        p = self.p
        to = p.first + j
        slot = lax.rem(p.k - to + p.H, p.H) - 1
        return remote(self.mine.at[j], self.came.at[slot], self.send.at[j], self.recv.at[slot],
                      2 * to + p.h, p.g)

    def arrival(self, slot):
        p = self.p
        return remote(self.came.at[slot], self.came.at[slot], self.send.at[0], self.recv.at[slot],
                      p.partner, p.g)

    def start(self):
        p = self.p
        for i in range(p.owners):
            j = p.far_owner(i)
            pl.when(p.mine != j)(lambda: self.copy(j).start())

    def total(self):
        total = self.mine[self.p.mine]
        for slot in range(self.p.H - 1):
            self.arrival(slot).wait_recv()
            total = total + self.came[slot]
        return total

    def finish(self):
        p = self.p
        for i in range(p.owners):
            j = p.far_owner(i)
            pl.when(p.mine != j)(lambda: self.copy(j).wait_send())


class Gather:
    def __init__(self, plan, full, line, group, relay):
        self.p, self.full, self.line, self.group, self.relay = plan, full, line, group, relay

    def slot(self, h, s, j):
        return self.full.at[:, self.p.chunk_rows(h, s, j)]

    def line_copy(self, chip):
        p = self.p
        slot = self.slot(p.h, p.s, p.mine)
        return remote(slot, slot, self.line[0].at[chip], self.line[1].at[p.mine], 2 * chip + p.h, p.g)

    def line_arrival(self, j):
        p = self.p
        slot = self.slot(p.h, p.s, j)
        return remote(slot, slot, self.line[0].at[0], self.line[1].at[j], p.partner, p.g)

    def group_copy(self, d, j, arriving):
        p = self.p
        n = (d - 1) * p.owners + j
        s = lax.rem(p.s + (p.gs - d if arriving else d), p.gs)
        slot = self.slot(p.h, s if arriving else p.s, j)
        return remote(slot, slot, self.group[0].at[n], self.group[1].at[n], p.t, p.g - p.s + s)

    def relay_copy(self, d, j, arriving):
        p = self.p
        n = d * p.owners + j
        s = lax.rem(p.s + p.gs - d, p.gs)
        slot = self.slot(1 - p.h if arriving else p.h, s, j)
        return remote(slot, slot, self.relay[0].at[n], self.relay[1].at[n], p.partner, p.g)

    def hand_on(self, j):
        for d in range(1, self.p.gs):
            self.group_copy(d, j, False).start()
        self.relay_copy(0, j, False).start()

    def start(self):
        p = self.p
        self.hand_on(p.mine)
        for i in range(p.H):
            chip = p.far_chip(i)
            pl.when(p.k != chip)(lambda: self.line_copy(chip).start())

    def forward(self):
        p = self.p
        for i in range(p.owners):
            j = p.near_owner(i)

            @pl.when(p.mine != j)
            def _():
                self.line_arrival(j).wait_recv()
                self.hand_on(j)
        for i in range(p.owners):
            for d in range(1, p.gs):
                j = p.near_owner(i)
                self.group_copy(d, j, True).wait_recv()
                self.relay_copy(d, j, False).start()

    def finish(self):
        p = self.p
        for d in range(p.gs):
            for j in range(p.owners):
                self.relay_copy(d, j, True).wait_recv()

    def drain(self):
        p = self.p

        @pl.when(p.owner)
        def _():
            for chip in range(p.H):
                pl.when(p.k != chip)(lambda: self.line_copy(chip).wait_send())
        for j in range(p.owners):
            for d in range(1, p.gs):
                self.group_copy(d, j, False).wait_send()
            for d in range(p.gs):
                self.relay_copy(d, j, False).wait_send()


def body(T, G, row_in, column_in, live_in, obj, probe_in, amp, tables_in, new_obj, new_probe,
         scal_in, scal, probe, tables, load_sem, pad, amp_raw, amps, win, terms, light_terms, acc,
         acc_light, edge, edge_light, light_full, light_whole, light_pair, light_whole_pair,
         light_mine, light_came, grad, grad_pair, grad_mine, grad_came, reach, own_s, own_r, side_s,
         side_r, amp_s, amp_r, scal_s, scal_r, edge_s, edge_r, pair_s, pair_r, light_s, light_r,
         grad_s, grad_r, line_s, line_r, group_s, group_r, relay_s, relay_r):
    t, g = lax.axis_index("tile"), lax.axis_index("group")
    R, B = obj.shape[1:]
    W = probe.shape[1]
    rows = pad.shape[2]
    spare, blocks = rows - W, W // B
    p = Plan(T, G, W)
    p.here(t, g)
    not_first, not_last = t > 0, t < T - 1

    def span(group):
        return pl.ds(pl.multiple_of(group * R, 8), R)

    own = pad.at[1, :, span(g)]
    loads = [pltpu.make_async_copy(src, dst, load_sem.at[i]) for i, (src, dst) in enumerate(
        [(obj, own), (probe_in, probe), (tables_in, tables)]
        + [(amp.at[0, :, b * B:(b + 1) * B], amp_raw.at[b]) for b in range(blocks)])]
    for load in loads:
        load.start()

    barrier = pltpu.get_barrier_semaphore()
    count = G - 1
    for j in range(1, G):
        pl.semaphore_signal(barrier, inc=1, device_id={"tile": t, "group": lax.rem(g + j, G)},
                            device_id_type=MESH)
    for d in (-1, 1, -2, 2):
        there = jnp.logical_and(t + d >= 0, t + d < T)

        @pl.when(there)
        def _():
            pl.semaphore_signal(barrier, inc=1, device_id={"tile": t + d, "group": g},
                                device_id_type=MESH)
        count = count + there.astype(jnp.int32)
    line = lax.broadcasted_iota(jnp.int32, scal_in.shape, 0)
    scal_in[...] = jnp.where(line == 0, row_in[0], jnp.where(line == 1, column_in[0], live_in[0]))
    pl.semaphore_wait(barrier, count)

    def to_peer(j, ch, arriving):
        peer = lax.rem(g + (G - j if arriving else j), G)
        slot = pad.at[1, ch, span(peer if arriving else g)]
        n = 2 * (j - 1) + ch
        return remote(slot if arriving else obj.at[ch], slot, own_s.at[n], own_r.at[n], t, peer)

    def to_side(j, ch, right, arriving):
        who = lax.rem(g + G - j, G)
        dst = pad.at[0 if right else 2, ch, span(who)]
        src = pad.at[1, ch, span(who)] if j else obj.at[ch]
        n = 4 * j + 2 * ch + int(right)
        return remote(dst if arriving else src, dst, side_s.at[n], side_r.at[n],
                      (t + 1 if right else t - 1) if not arriving else (t - 1 if right else t + 1), g)

    def amp_copy(j, arriving):
        peer = lax.rem(g + (G - j if arriving else j), G)
        slot = amps.at[peer if arriving else g]
        return remote(slot, slot, amp_s.at[j - 1], amp_r.at[j - 1], t, peer)

    def scal_copy(j, arriving):
        peer = lax.rem(g + (G - j if arriving else j), G)
        slot = scal.at[peer if arriving else g]
        return remote(slot if arriving else scal_in, slot, scal_s.at[j - 1], scal_r.at[j - 1], t, peer)

    def edge_copy(src, dst, right, base, arriving):
        n = base + int(right)
        side = dst.at[0 if right else 1]
        if arriving:
            return remote(side, side, edge_s.at[n], edge_r.at[n], t - 1 if right else t + 1, g)
        return remote(src.at[2 if right else 0], side, edge_s.at[n], edge_r.at[n],
                      t + 1 if right else t - 1, g)

    def pair_copy(src, dst, n):
        return remote(src, dst, pair_s.at[n], pair_r.at[n], p.partner, g)

    def to_sides(j, ch):
        pl.when(not_first)(lambda: to_side(j, ch, False, False).start())
        pl.when(not_last)(lambda: to_side(j, ch, True, False).start())

    for ch in range(2):
        for j in range(1, G):
            to_peer(j, ch, False).start()
        to_sides(0, ch)
    for j in range(1, G):
        scal_copy(j, False).start()

    known, rounds = 1, []
    while known < p.H - 1:
        rounds.append(known)
        known *= 2

    def ends(d):
        return [(p.k - d, p.k >= d), (p.k + d, p.k + d < p.H)]

    def tell(i):
        for chip, there in ends(rounds[i]):
            @pl.when(there)
            def _():
                pl.semaphore_signal(reach.at[i], inc=1,
                                    device_id={"tile": 2 * chip + p.h, "group": g}, device_id_type=MESH)

    def hear(i):
        (_, below), (_, above) = ends(rounds[i])
        pl.semaphore_wait(reach.at[i], below.astype(jnp.int32) + above.astype(jnp.int32))

    tell(0)
    scal[g] = scal_in[...]

    for load in loads[3:]:
        load.wait()
    n = W // 2
    a = cat([cat([amp_raw[b, pl.ds(q, n, stride=2), :] for q in range(2)], 0) for b in range(blocks)], 1)
    at = lax.broadcasted_iota(jnp.int32, (W, W), 1)
    at = jnp.where(at < n, 2 * at, 2 * at - (W - 1))
    order = jnp.where(lax.broadcasted_iota(jnp.int32, (W, W), 0) == at, 1.0, 0.0).astype(BF16)
    top = a.astype(BF16)
    rest = a - top.astype(F32)
    middle, low = split(rest)
    amps[g] = mm(top, order) + (mm(middle, order) + mm(low, order))
    for j in range(1, G):
        amp_copy(j, False).start()

    @pl.when(t == 0)
    def _():
        pad[0] = jnp.zeros(pad.shape[1:], F32)
        edge[0] = jnp.zeros(edge.shape[1:], F32)
        edge_light[0] = jnp.zeros(edge_light.shape[1:], F32)

    @pl.when(t == T - 1)
    def _():
        pad[2] = jnp.zeros(pad.shape[1:], F32)
        edge[1] = jnp.zeros(edge.shape[1:], F32)
        edge_light[1] = jnp.zeros(edge_light.shape[1:], F32)

    terms[:, :, 0:spare] = jnp.zeros((2, blocks, spare, B), F32)
    terms[:, :, spare + W:] = jnp.zeros((2, blocks, spare, B), F32)
    light_terms[:, 0:spare] = jnp.zeros((blocks, spare, B), F32)
    light_terms[:, spare + W:] = jnp.zeros((blocks, spare, B), F32)

    def hold(ref, value):
        for b in range(blocks):
            ref[b, spare:spare + W] = value[:, b * B:(b + 1) * B]

    for load in loads[:3]:
        load.wait()
    probe_light = probe[0] * probe[0] + probe[1] * probe[1]
    hold(light_terms, probe_light)
    light_max = jnp.max(probe_light) + 1e-06

    for ch in range(2):
        for j in range(1, G):
            to_peer(j, ch, True).wait_recv()
            to_sides(j, ch)
    for i in range(len(rounds)):
        hear(i)
        if i + 1 < len(rounds):
            tell(i + 1)
    for j in range(1, G):
        scal_copy(j, True).wait_recv()
    for j in range(G):
        for ch in range(2):
            pl.when(not_last)(lambda: to_side(j, ch, False, True).wait_recv())
            pl.when(not_first)(lambda: to_side(j, ch, True, True).wait_recv())

    def numbers(k):
        return scal[k, 0, 0], scal[k, 1, 0], scal[k, 2, 0].astype(F32)

    def placed(ref, row, column):
        first = g * R + spare - row
        pieces = [ref[b, pl.ds(first, R), :] for b in range(blocks)]
        wide = cat(pieces + [jnp.zeros((R, 3 * B - W), F32)], 1)
        wide = pltpu.roll(wide, column, 1)
        return [wide[:, b * B:(b + 1) * B] for b in range(3)]

    def look(k, first):
        row, column, weight = numbers(k)
        for ch in range(2):
            wide = cat([pad[b, ch, pl.ds(row, W), :] for b in range(3)], 1)
            win[k, ch] = pltpu.roll(wide, lax.rem(3 * B - column, 3 * B), 1)[:, 0:W]
        for b, piece in enumerate(placed(light_terms, row, column)):
            piece = weight * piece
            acc_light[b] = piece if first else acc_light[b] + piece
        light = weight * (win[k, 0] * win[k, 0] + win[k, 1] * win[k, 1])
        light_full[...] = light if first else light_full[...] + light

    def position(k, first):
        row, column, weight = numbers(k)
        wr, wi = win[k, 0], win[k, 1]
        pr, pi = probe[0], probe[1]
        freq = fold_in(pr * wr - pi * wi, pr * wi + pi * wr, tables)
        scaled = []
        for q in range(2):
            fr, fi = freq[q][:, :n], freq[q][:, n:]
            factor = weight - (weight * amps[k, :, q * n:(q + 1) * n]) * lax.rsqrt(
                jnp.maximum(fr * fr + fi * fi, 0.0625))
            scaled.append(cat([fr * factor, fi * factor], 1))
        mr, mi = fold_out(*scaled, tables)
        pr, pi = probe[0], probe[1]
        wr, wi = win[k, 0], win[k, 1]
        for ch, value in enumerate((wr * mr + wi * mi, wr * mi - wi * mr)):
            grad[ch] = value if first else grad[ch] + value
        hold(terms.at[0], pr * mr + pi * mi)
        hold(terms.at[1], pr * mi - pi * mr)

    def add_terms(k, first):
        row, column, _ = numbers(k)
        for ch in range(2):
            for b, piece in enumerate(placed(terms.at[ch], row, column)):
                acc[b, ch] = piece if first else acc[b, ch] + piece

    def peers(f):
        if G == 2:
            f(1)
        elif G > 2:
            pl.loop(1, G)(f)

    look(g, True)
    peers(lambda j: look(lax.rem(g + G - j, G), False))
    light_whole[...] = jnp.sum(light_full[...].reshape(W // 8, 8, W), axis=0)
    light_pairs = [pair_copy(light_full.at[p.rows(1 - p.h, p.s)], light_pair, 0),
                   pair_copy(light_whole, light_whole_pair, 1)]
    for copy in light_pairs:
        copy.start()
    pl.when(not_first)(lambda: edge_copy(acc_light, edge_light, False, 0, False).start())
    pl.when(not_last)(lambda: edge_copy(acc_light, edge_light, True, 0, False).start())

    position(g, True)
    add_terms(g, True)

    for copy in light_pairs:
        copy.wait()
    whole = light_whole[...] + light_whole_pair[...]
    for j in range(p.owners):
        light_mine[j, 0:p.chunk] = (light_full[p.chunk_rows(p.h, p.s, j), :]
                                    + light_pair[j * p.chunk:(j + 1) * p.chunk, :])
        light_mine[j, p.chunk:] = whole
    light_red = Reduce(p, light_mine, light_came, light_s, light_r)
    light_red.start()

    def peer_position(j):
        amp_copy(j, True).wait_recv()
        k = lax.rem(g + G - j, G)
        position(k, False)
        if G > 2:
            add_terms(k, False)

    peers(peer_position)
    grad_pairs = pair_copy(grad.at[:, p.rows(1 - p.h, p.s)], grad_pair, 2)
    grad_pairs.start()
    if G == 2:
        add_terms(1 - g, False)
    grad_pairs.wait()
    for j in range(p.owners):
        grad_mine[j] = (grad[:, p.chunk_rows(p.h, p.s, j), :]
                        + grad_pair[:, j * p.chunk:(j + 1) * p.chunk, :])
    grad_red = Reduce(p, grad_mine, grad_came, grad_s, grad_r)
    grad_red.start()
    pl.when(not_first)(lambda: edge_copy(acc, edge, False, 2, False).start())
    pl.when(not_last)(lambda: edge_copy(acc, edge, True, 2, False).start())

    spread = Gather(p, new_probe, (line_s, line_r), (group_s, group_r), (relay_s, relay_r))

    @pl.when(p.owner)
    def _():
        light = light_red.total()
        mean = jnp.sum(light[p.chunk:]) * (1.0 / (W * W))
        below = 1.0 / (light[:p.chunk] + 0.25 * mean + 1e-05)
        here = p.chunk_rows(p.h, p.s, p.mine)
        total = grad_red.total()
        for ch in range(2):
            new_probe[ch, here, :] = probe[ch, here, :] - total[ch] * below
        spread.start()

    spread.forward()
    for src, dst, base in ((acc_light, edge_light, 0), (acc, edge, 2)):
        pl.when(not_last)(lambda: edge_copy(src, dst, False, base, True).wait_recv())
        pl.when(not_first)(lambda: edge_copy(src, dst, True, base, True).wait_recv())
    below = 1.0 / (acc_light[1] + edge_light[0] + edge_light[1] + 0.25 * light_max)
    for ch in range(2):
        new_obj[ch] = own[ch] - (acc[1, ch] + edge[0, ch] + edge[1, ch]) * below

    for j in range(1, G):
        for ch in range(2):
            to_peer(j, ch, False).wait_send()
        amp_copy(j, False).wait_send()
        scal_copy(j, False).wait_send()
    for j in range(G):
        for ch in range(2):
            pl.when(not_first)(lambda: to_side(j, ch, False, False).wait_send())
            pl.when(not_last)(lambda: to_side(j, ch, True, False).wait_send())
    for src, dst, base in ((acc_light, edge_light, 0), (acc, edge, 2)):
        pl.when(not_first)(lambda: edge_copy(src, dst, False, base, False).wait_send())
        pl.when(not_last)(lambda: edge_copy(src, dst, True, base, False).wait_send())
    light_red.finish()
    grad_red.finish()
    spread.finish()
    spread.drain()


def put(obj, probe, obj_out, probe_out, sems):
    copies = [pltpu.make_async_copy(obj, obj_out, sems.at[0]),
              pltpu.make_async_copy(probe, probe_out, sems.at[1])]
    for copy in copies:
        copy.start()
    for copy in copies:
        copy.wait()


def local(T, G, object_field, probe_field, amplitudes, row_start, column_start, live_slots):
    R, B = object_field.shape[1:]
    W = probe_field.shape[1]
    rows = R * G
    p = Plan(T, G, W)
    tables = dft_tables(W)
    spare, blocks = rows - W, W // B
    dma = lambda n: pltpu.SemaphoreType.DMA((max(n, 1),))
    vm = lambda *shape: pltpu.VMEM(shape, F32)

    vmem_limit = 67043328 - 4 * (object_field.size + probe_field.size) - 65536
    smem = pl.BlockSpec(memory_space=pltpu.SMEM)
    hbm = pl.BlockSpec(memory_space=pltpu.HBM)
    vmem = pl.BlockSpec(memory_space=pltpu.VMEM)
    new_obj, new_probe = pl.pallas_call(
        functools.partial(body, T, G),
        out_shape=(pltpu.VMEM(object_field.shape, F32), pltpu.VMEM(probe_field.shape, F32)),
        in_specs=[smem] * 3 + [hbm] * 4,
        out_specs=(vmem, vmem),
        scratch_shapes=[
            pltpu.VMEM((8, 128), jnp.int32),
            pltpu.VMEM((G, 8, 128), jnp.int32),
            vm(2, W, W),
            pltpu.VMEM(tables.shape, BF16),
            dma(3 + blocks),
            vm(3, 2, rows, B),
            vm(blocks, W, B), vm(G, W, W), vm(G, 2, W, W),
            vm(2, blocks, W + 2 * spare, B), vm(blocks, W + 2 * spare, B),
            vm(3, 2, R, B), vm(3, R, B), vm(2, 2, R, B), vm(2, R, B),
            vm(W, W), vm(8, W), vm(p.part, W), vm(8, W),
            vm(p.owners, p.chunk + 8, W), vm(p.H - 1, p.chunk + 8, W),
            vm(2, W, W), vm(2, p.part, W),
            vm(p.owners, 2, p.chunk, W), vm(p.H - 1, 2, p.chunk, W),
            pltpu.SemaphoreType.REGULAR((max(p.H.bit_length(), 1),)),
            dma(2 * G - 2), dma(2 * G - 2), dma(4 * G), dma(4 * G), dma(G - 1), dma(G - 1),
            dma(G - 1), dma(G - 1), dma(4), dma(4), dma(3), dma(3),
            dma(p.owners), dma(p.H - 1), dma(p.owners), dma(p.H - 1),
            dma(p.H), dma(p.owners), dma((p.gs - 1) * p.owners), dma((p.gs - 1) * p.owners),
            dma(p.gs * p.owners), dma(p.gs * p.owners),
        ],
        compiler_params=pltpu.CompilerParams(
            collective_id=0, has_side_effects=True, vmem_limit_bytes=vmem_limit),
    )(row_start, column_start, live_slots, object_field, probe_field, amplitudes, tables)
    anywhere = pl.BlockSpec(memory_space=pl.ANY)
    return pl.pallas_call(
        put,
        out_shape=(jax.ShapeDtypeStruct(object_field.shape, F32),
                   jax.ShapeDtypeStruct(probe_field.shape, F32)),
        in_specs=[vmem] * 2,
        out_specs=(anywhere, anywhere),
        scratch_shapes=[dma(2)],
        compiler_params=pltpu.CompilerParams(vmem_limit_bytes=1024 * 1024),
    )(new_obj, new_probe)


def solution(mesh):
    return jax.shard_map(
        functools.partial(local, mesh.shape["tile"], mesh.shape["group"]),
        mesh=mesh,
        in_specs=(
            P(None, "group", "tile"),
            P(),
            P(("tile", "group"), None, None),
            P(("tile", "group")),
            P(("tile", "group")),
            P(("tile", "group")),
        ),
        out_specs=(P(None, "group", "tile"), P()),
        check_vma=False,
    )
```

```python
import functools
import math

import jax
import jax.numpy as jnp
import numpy as np
from jax import lax
from jax.experimental import pallas as pl
from jax.experimental.pallas import tpu as pltpu
from jax.sharding import PartitionSpec as P

MESH = pl.DeviceIdType.MESH
F32 = jnp.float32
BF16 = jnp.bfloat16


def dft_tables(length):
    k = np.arange(length // 2)
    even = (2 * np.outer(k, k)) % length
    odd = np.outer(2 * k + 1, k) % length
    tables = []
    for turns in (even, odd):
        angles = 2.0 * math.pi / length * turns
        cos, sin = np.cos(angles) / math.sqrt(length), np.sin(angles) / math.sqrt(length)
        full = np.block([[cos, sin], [-sin, cos]])
        tables += [full, full.T]
    full = np.stack(tables).astype(np.float32)
    head = full.astype(BF16)
    tail = (full - head.astype(np.float32)).astype(BF16)
    return np.stack([head, tail], axis=1)


EVEN, EVEN_T, ODD, ODD_T = range(4)


def split(x):
    head = x.astype(BF16)
    return head, (x - head.astype(F32)).astype(BF16)


def mm(a, b):
    return jnp.dot(a, b, preferred_element_type=F32)


def cat(parts, axis):
    return jnp.concatenate(parts, axis=axis)


def table_left(table, x):
    head, tail = split(x)
    return mm(cat([table[0], table[0], table[1]], 1), cat([head, tail, head], 0))


def table_right(x, table):
    head, tail = split(x)
    return mm(cat([head, tail, head], 1), cat([table[0], table[0], table[1]], 0))


def fold_in(xr, xi, tables):
    n = xr.shape[0] // 2
    a = cat([xr[:n] + xr[n:], xi[:n] + xi[n:]], 0)
    b = cat([xr[:n] - xr[n:], xi[:n] - xi[n:]], 0)
    halves = table_left(tables[EVEN], a), table_left(tables[ODD], b)

    def sides(sign):
        rows = []
        for y in halves:
            yr, yi = y[:n], y[n:]
            rows.append(cat([yr[:, :n] + sign * yr[:, n:], yi[:, :n] + sign * yi[:, n:]], 1))
        return cat(rows, 0)

    return table_right(sides(1), tables[EVEN_T]), table_right(sides(-1), tables[ODD_T])


def fold_out(even, odd, tables):
    n = even.shape[0] // 2
    e, o = table_right(even, tables[EVEN]), table_right(odd, tables[ODD])
    plus, minus = e + o, e - o
    halves = []
    for q, table in ((0, tables[EVEN_T]), (1, tables[ODD_T])):
        r = slice(q * n, (q + 1) * n)
        halves.append(table_left(table, cat(
            [cat([plus[r, :n], minus[r, :n]], 1), cat([plus[r, n:], minus[r, n:]], 1)], 0)))
    plus, minus = halves[0] + halves[1], halves[0] - halves[1]
    return cat([plus[:n], minus[:n]], 0), cat([plus[n:], minus[n:]], 0)


def remote(src, dst, send, recv, tile, group):
    return pltpu.make_async_remote_copy(
        src_ref=src, dst_ref=dst, send_sem=send, recv_sem=recv,
        device_id={"tile": tile, "group": group}, device_id_type=MESH,
    )


class Plan:
    def __init__(self, T, G, W):
        self.H = T // 2
        self.owners = self.H // 2 if self.H % 4 == 0 else self.H
        self.first = (self.H - self.owners) // 2
        self.gs = max(n for n in range(1, G + 1) if G % n == 0 and n * self.owners * 8 <= W // 2)
        self.W, self.half = W, W // 2
        self.part = self.half // self.gs
        self.chunk = self.part // self.owners

    def here(self, t, g):
        self.t, self.g = t, g
        self.k, self.h = lax.div(t, 2), lax.rem(t, 2)
        self.partner = t + 1 - 2 * self.h
        self.s = lax.rem(g, self.gs)
        self.mine = self.k - self.first
        self.low = self.k < self.H // 2
        self.owner = jnp.logical_and(self.mine >= 0, self.mine < self.owners)

    def rows(self, h, s):
        return pl.ds(pl.multiple_of(h * self.half + s * self.part, 8), self.part)

    def chunk_rows(self, h, s, j):
        return pl.ds(pl.multiple_of(h * self.half + s * self.part + j * self.chunk, 8), self.chunk)

    def far_owner(self, i):
        return lax.rem(i + jnp.where(self.low, self.owners // 2, 0), self.owners)

    def near_owner(self, i):
        return jnp.where(self.low, i, self.owners - 1 - i)

    def far_chip(self, i):
        return jnp.where(self.low, self.H - 1 - i, i)


class Reduce:
    def __init__(self, plan, mine, came, sems):
        self.p, self.mine, self.came, self.sems = plan, mine, came, sems

    def copy(self, j):
        p = self.p
        to = p.first + j
        slot = lax.rem(p.k - to + p.H, p.H) - 1
        return remote(self.mine.at[j], self.came.at[slot], self.sems.at[0], self.sems.at[1],
                      2 * to + p.h, p.g)

    def bytes_of(self, ref):
        return remote(ref, ref, self.sems.at[0], self.sems.at[1], self.p.partner, self.p.g)

    def start(self):
        p = self.p
        for i in range(p.owners):
            j = p.far_owner(i)
            pl.when(p.mine != j)(lambda: self.copy(j).start())

    def total(self):
        self.bytes_of(self.came).wait_recv()
        total = self.mine[self.p.mine]
        for slot in range(self.p.H - 1):
            total = total + self.came[slot]
        return total

    def finish(self):
        p = self.p
        pl.when(p.owner)(lambda: self.bytes_of(self.mine.at[0:p.owners - 1]).wait_send())
        pl.when(jnp.logical_not(p.owner))(lambda: self.bytes_of(self.mine).wait_send())


class Gather:
    def __init__(self, plan, full, spare, sent, line, group, relay):
        self.p, self.full, self.spare, self.sent = plan, full, spare, sent
        self.line, self.group, self.relay = line, group, relay

    def slot(self, h, s, j):
        return self.full.at[h, s, j]

    def line_copy(self, chip):
        p = self.p
        slot = self.slot(p.h, p.s, p.mine)
        return remote(slot, slot, self.sent.at[0], self.line.at[p.mine], 2 * chip + p.h, p.g)

    def line_arrival(self, j):
        p = self.p
        slot = self.slot(p.h, p.s, j)
        return remote(slot, slot, self.sent.at[0], self.line.at[j], p.partner, p.g)

    def group_copy(self, d, j, arriving):
        p = self.p
        n = (d - 1) * p.owners + j
        s = lax.rem(p.s + (p.gs - d if arriving else d), p.gs)
        slot = self.slot(p.h, s if arriving else p.s, j)
        return remote(slot, slot, self.sent.at[1], self.group.at[n], p.t, p.g - p.s + s)

    def relay_copy(self, d, j):
        p = self.p
        slot = self.slot(p.h, lax.rem(p.s + p.gs - d, p.gs), j)
        return remote(slot, slot, self.sent.at[2], self.relay.at[0], p.partner, p.g)

    def bytes_of(self, ref, n):
        return remote(ref, ref, self.sent.at[n], self.relay.at[0], self.p.partner, self.p.g)

    def hand_on(self, j):
        for d in range(1, self.p.gs):
            self.group_copy(d, j, False).start()
        self.relay_copy(0, j).start()

    def start(self):
        p = self.p
        self.hand_on(p.mine)
        for i in range(p.H):
            chip = p.far_chip(i)
            pl.when(p.k != chip)(lambda: self.line_copy(chip).start())

    def forward(self):
        p = self.p
        for i in range(p.owners):
            j = p.near_owner(i)

            @pl.when(p.mine != j)
            def _():
                self.line_arrival(j).wait_recv()
                self.hand_on(j)
        for i in range(p.owners):
            for d in range(1, p.gs):
                j = p.near_owner(i)
                self.group_copy(d, j, True).wait_recv()
                self.relay_copy(d, j).start()

    def finish(self):
        self.bytes_of(self.full.at[1 - self.p.h], 2).wait_recv()

    def drain(self):
        p = self.p
        pl.when(p.owner)(lambda: self.bytes_of(self.spare, 0).wait_send())
        if p.gs > 1:
            self.bytes_of(self.full.at[0, 0:p.gs - 1], 1).wait_send()
        self.bytes_of(self.full.at[0], 2).wait_send()


def body(T, G, row_in, column_in, live_in, obj, probe_in, amp, tables_in, new_obj, new_probe,
         scal_in, scal, probe, tables, load_sem, pad, amp_raw, amps, win, terms, light_terms, acc,
         acc_light, edge, edge_light, light_full, light_whole, light_pair, light_mine, light_came,
         grad, grad_pair, grad_mine, grad_came, full, reach, own_s, own_r, side_s, side_r, amp_s,
         amp_r, scal_s, edge_s, edge_r, pair_s, pair_r, light_s, grad_s, sent, line_r, group_r,
         relay_r):
    t, g = lax.axis_index("tile"), lax.axis_index("group")
    R, B = obj.shape[1:]
    W = probe.shape[1]
    rows = pad.shape[2]
    spare, blocks = rows - W, W // B
    p = Plan(T, G, W)
    p.here(t, g)
    not_first, not_last = t > 0, t < T - 1

    def span(group):
        return pl.ds(pl.multiple_of(group * R, 8), R)

    own = pad.at[1, :, span(g)]
    loads = [pltpu.make_async_copy(src, dst, load_sem.at[i]) for i, (src, dst) in enumerate(
        [(obj, own), (probe_in, probe), (tables_in, tables)])]
    amp_loads = [pltpu.make_async_copy(amp.at[0, :, b * B:(b + 1) * B], amp_raw.at[b], load_sem.at[3])
                 for b in range(blocks)]
    for load in amp_loads + loads:
        load.start()

    barrier = pltpu.get_barrier_semaphore()
    count = G - 1
    for j in range(1, G):
        pl.semaphore_signal(barrier, inc=1, device_id={"tile": t, "group": lax.rem(g + j, G)},
                            device_id_type=MESH)
    for d in (-1, 1, -2, 2):
        there = jnp.logical_and(t + d >= 0, t + d < T)

        @pl.when(there)
        def _():
            pl.semaphore_signal(barrier, inc=1, device_id={"tile": t + d, "group": g},
                                device_id_type=MESH)
        count = count + there.astype(jnp.int32)
    line = lax.broadcasted_iota(jnp.int32, scal_in.shape, 0)
    scal_in[...] = jnp.where(line == 0, row_in[0], jnp.where(line == 1, column_in[0], live_in[0]))
    pl.semaphore_wait(barrier, count)

    cut_row = R // 16 * 8
    pieces = [(0, cut_row), (cut_row, R - cut_row)] if cut_row else [(0, R)]

    def piece(group, q):
        return pl.ds(pl.multiple_of(group * R + pieces[q][0], 8), pieces[q][1])

    def to_peer(j, ch, q, arriving):
        peer = lax.rem(g + (G - j if arriving else j), G)
        slot = pad.at[1, ch, piece(peer if arriving else g, q)]
        n = (2 * (j - 1) + ch) * len(pieces) + q
        src = slot if arriving else obj.at[ch, pieces[q][0]:pieces[q][0] + pieces[q][1]]
        return remote(src, slot, own_s.at[0], own_r.at[n], t, peer)

    def to_side(ch, right, src, rows_of):
        dst = pad.at[0 if right else 2, ch, rows_of]
        return remote(src, dst, side_s.at[int(right)], side_r.at[2 * ch + int(right)],
                      t + 1 if right else t - 1, g)

    def side_bytes(ref, ch, right):
        return remote(ref, ref, side_s.at[int(right)], side_r.at[2 * ch + int(right)], p.partner, g)

    def amp_copy(j, arriving):
        peer = lax.rem(g + (G - j if arriving else j), G)
        slot = amps.at[peer if arriving else g]
        return remote(slot, slot, amp_s.at[0], amp_r.at[j - 1], t, peer)

    def scal_copy(j):
        return remote(scal_in, scal.at[g], scal_s.at[0], scal_s.at[1], t, lax.rem(g + j, G))

    def bytes_of(ref, send, recv):
        return remote(ref, ref, send, recv, p.partner, g)

    def edge_copy(src, dst, right, base, arriving):
        n = base + int(right)
        side = dst.at[0 if right else 1]
        if arriving:
            return remote(side, side, edge_s.at[int(right)], edge_r.at[n], t - 1 if right else t + 1, g)
        return remote(src.at[2 if right else 0], side, edge_s.at[int(right)], edge_r.at[n],
                      t + 1 if right else t - 1, g)

    def edges_sent(src, dst, base):
        pl.when(not_first)(lambda: edge_copy(src, dst, False, base, False).wait_send())
        pl.when(not_last)(lambda: edge_copy(src, dst, True, base, False).wait_send())

    def pair_copy(src, dst, n):
        return remote(src, dst, pair_s.at[n], pair_r.at[n], p.partner, g)

    def to_sides(ch, src, rows_of):
        pl.when(not_first)(lambda: to_side(ch, False, src, rows_of).start())
        pl.when(not_last)(lambda: to_side(ch, True, src, rows_of).start())

    for ch in range(2):
        for q in range(len(pieces)):
            for j in range(1, G):
                to_peer(j, ch, q, False).start()
        to_sides(ch, obj.at[ch], span(g))
    for j in range(1, G):
        scal_copy(j).start()

    known, rounds = 1, []
    while known < p.H - 1:
        rounds.append(known)
        known *= 2

    def ends(d):
        return [(p.k - d, p.k >= d), (p.k + d, p.k + d < p.H)]

    def tell(i):
        for chip, there in ends(rounds[i]):
            @pl.when(there)
            def _():
                pl.semaphore_signal(reach.at[i], inc=1,
                                    device_id={"tile": 2 * chip + p.h, "group": g}, device_id_type=MESH)

    def hear(i):
        (_, below), (_, above) = ends(rounds[i])
        pl.semaphore_wait(reach.at[i], below.astype(jnp.int32) + above.astype(jnp.int32))

    tell(0)
    scal[g] = scal_in[...]

    pltpu.make_async_copy(amp_raw, amp_raw, load_sem.at[3]).wait()
    n = W // 2
    a = cat([cat([amp_raw[b, pl.ds(q, n, stride=2), :] for q in range(2)], 0) for b in range(blocks)], 1)
    at = lax.broadcasted_iota(jnp.int32, (W, W), 1)
    at = jnp.where(at < n, 2 * at, 2 * at - (W - 1))
    order = jnp.where(lax.broadcasted_iota(jnp.int32, (W, W), 0) == at, 1.0, 0.0).astype(BF16)
    top = a.astype(BF16)
    rest = a - top.astype(F32)
    middle, low = split(rest)
    amps[g] = mm(top, order) + (mm(middle, order) + mm(low, order))
    for j in range(1, G):
        amp_copy(j, False).start()

    @pl.when(t == 0)
    def _():
        pad[0] = jnp.zeros(pad.shape[1:], F32)
        edge[0] = jnp.zeros(edge.shape[1:], F32)
        edge_light[0] = jnp.zeros(edge_light.shape[1:], F32)

    @pl.when(t == T - 1)
    def _():
        pad[2] = jnp.zeros(pad.shape[1:], F32)
        edge[1] = jnp.zeros(edge.shape[1:], F32)
        edge_light[1] = jnp.zeros(edge_light.shape[1:], F32)

    terms[:, :, 0:spare] = jnp.zeros((2, blocks, spare, B), F32)
    terms[:, :, spare + W:] = jnp.zeros((2, blocks, spare, B), F32)
    light_terms[:, 0:spare] = jnp.zeros((blocks, spare, B), F32)
    light_terms[:, spare + W:] = jnp.zeros((blocks, spare, B), F32)

    def hold(ref, value):
        for b in range(blocks):
            ref[b, spare:spare + W] = value[:, b * B:(b + 1) * B]

    for load in loads:
        load.wait()
    probe_light = probe[0] * probe[0] + probe[1] * probe[1]
    hold(light_terms, probe_light)
    light_max = jnp.max(probe_light) + 1e-06

    for ch in range(2):
        for q in range(len(pieces)):
            for j in range(1, G):
                to_peer(j, ch, q, True).wait_recv()
                rows_of = piece(lax.rem(g + G - j, G), q)
                to_sides(ch, pad.at[1, ch, rows_of], rows_of)
    if G > 1:
        bytes_of(scal.at[0:G - 1], scal_s.at[0], scal_s.at[1]).wait_recv()

    def next_round(i):
        hear(i)
        if i + 1 < len(rounds):
            tell(i + 1)

    def numbers(k):
        return scal[k, 0, 0], scal[k, 1, 0], scal[k, 2, 0].astype(F32)

    lane = lax.broadcasted_iota(jnp.int32, (8, B), 1)[0:1]

    def placed(ref, row, column):
        first = g * R + spare - row
        shift = lax.rem(column, B)
        stay = lane >= column
        pieces = [pltpu.roll(ref[b, pl.ds(first, R), :], shift, 1) for b in range(blocks)]
        out = [jnp.where(stay, pieces[0], 0.0)]
        out += [jnp.where(stay, pieces[b], pieces[b - 1]) for b in range(1, blocks)]
        return out + [jnp.where(stay, 0.0, pieces[-1])]

    def cut(k, ch):
        row, column, _ = numbers(k)
        shift = lax.rem(B - lax.rem(column, B), B)
        stay = lane < B - column
        pieces = [pltpu.roll(pad[b, ch, pl.ds(row, W), :], shift, 1) for b in range(blocks + 1)]
        for b in range(blocks):
            win[k, ch, :, b * B:(b + 1) * B] = jnp.where(stay, pieces[b], pieces[b + 1])

    def place_light(k, first):
        row, column, weight = numbers(k)
        for b, piece in enumerate(placed(light_terms, row, column)):
            piece = weight * piece
            acc_light[b] = piece if first else acc_light[b] + piece

    def look(k, first):
        weight = numbers(k)[2]
        light = weight * (win[k, 0] * win[k, 0] + win[k, 1] * win[k, 1])
        light_full[...] = light if first else light_full[...] + light

    def position(k, first):
        row, column, weight = numbers(k)
        wr, wi = win[k, 0], win[k, 1]
        pr, pi = probe[0], probe[1]
        freq = fold_in(pr * wr - pi * wi, pr * wi + pi * wr, tables)
        scaled = []
        for q in range(2):
            fr, fi = freq[q][:, :n], freq[q][:, n:]
            factor = weight - (weight * amps[k, :, q * n:(q + 1) * n]) * lax.rsqrt(
                jnp.maximum(fr * fr + fi * fi, 0.0625))
            scaled.append(cat([fr * factor, fi * factor], 1))
        mr, mi = fold_out(*scaled, tables)
        pr, pi = probe[0], probe[1]
        wr, wi = win[k, 0], win[k, 1]
        for ch, value in enumerate((wr * mr + wi * mi, wr * mi - wi * mr)):
            grad[ch] = value if first else grad[ch] + value
        hold(terms.at[0], pr * mr + pi * mi)
        hold(terms.at[1], pr * mi - pi * mr)

    def add_terms(k, first):
        row, column, _ = numbers(k)
        for ch in range(2):
            for b, piece in enumerate(placed(terms.at[ch], row, column)):
                acc[b, ch] = piece if first else acc[b, ch] + piece

    def peers(f):
        if G == 2:
            f(1)
        elif G > 2:
            pl.loop(1, G)(f)

    place_light(g, True)
    peers(lambda j: place_light(lax.rem(g + G - j, G), False))
    next_round(0)
    for ch in range(2):
        pl.when(not_last)(lambda: side_bytes(pad.at[2, ch], ch, False).wait_recv())
        pl.when(not_first)(lambda: side_bytes(pad.at[0, ch], ch, True).wait_recv())
    for ch in range(2):
        cut(g, ch)
        peers(lambda j: cut(lax.rem(g + G - j, G), ch))
    look(g, True)
    peers(lambda j: look(lax.rem(g + G - j, G), False))
    light_whole[...] = jnp.sum(light_full[...].reshape(W // 8, 8, W), axis=0)
    pair_copy(light_full.at[p.rows(1 - p.h, p.s)], light_pair.at[0:p.part], 0).start()
    pair_copy(light_whole, light_pair.at[p.part:p.part + 8], 0).start()
    pl.when(not_first)(lambda: edge_copy(acc_light, edge_light, False, 0, False).start())
    pl.when(not_last)(lambda: edge_copy(acc_light, edge_light, True, 0, False).start())
    if len(rounds) > 1:
        next_round(1)

    position(g, True)
    add_terms(g, True)

    for i in range(2, len(rounds)):
        next_round(i)
    pair_copy(light_pair, light_pair, 0).wait()
    whole = light_whole[...] + light_pair[p.part:, :]
    for j in range(p.owners):
        light_mine[j, 0:p.chunk] = (light_full[p.chunk_rows(p.h, p.s, j), :]
                                    + light_pair[j * p.chunk:(j + 1) * p.chunk, :])
        light_mine[j, p.chunk:] = whole
    light_red = Reduce(p, light_mine, light_came, light_s)
    light_red.start()

    def peer_position(j):
        amp_copy(j, True).wait_recv()
        k = lax.rem(g + G - j, G)
        position(k, False)
        if G > 2:
            add_terms(k, False)

    peers(peer_position)
    grad_pairs = pair_copy(grad.at[:, p.rows(1 - p.h, p.s)], grad_pair, 1)
    grad_pairs.start()
    if G == 2:
        add_terms(1 - g, False)
    grad_pairs.wait()
    for j in range(p.owners):
        grad_mine[j] = (grad[:, p.chunk_rows(p.h, p.s, j), :]
                        + grad_pair[:, j * p.chunk:(j + 1) * p.chunk, :])
    grad_red = Reduce(p, grad_mine, grad_came, grad_s)
    grad_red.start()
    edges_sent(acc_light, edge_light, 0)
    pl.when(not_first)(lambda: edge_copy(acc, edge, False, 2, False).start())
    pl.when(not_last)(lambda: edge_copy(acc, edge, True, 2, False).start())

    spread = Gather(p, full, grad_came, sent, line_r, group_r, relay_r)

    @pl.when(p.owner)
    def _():
        light = light_red.total()
        mean = jnp.sum(light[p.chunk:]) * (1.0 / (W * W))
        below = 1.0 / (light[:p.chunk] + 0.25 * mean + 1e-05)
        here = p.chunk_rows(p.h, p.s, p.mine)
        total = grad_red.total()
        for ch in range(2):
            full[p.h, p.s, p.mine, ch] = probe[ch, here, :] - total[ch] * below
        spread.start()

    spread.forward()
    for src, dst, base in ((acc_light, edge_light, 0), (acc, edge, 2)):
        pl.when(not_last)(lambda: edge_copy(src, dst, False, base, True).wait_recv())
        pl.when(not_first)(lambda: edge_copy(src, dst, True, base, True).wait_recv())
    below = 1.0 / (acc_light[1] + edge_light[0] + edge_light[1] + 0.25 * light_max)
    for ch in range(2):
        new_obj[ch] = own[ch] - (acc[1, ch] + edge[0, ch] + edge[1, ch]) * below

    if G > 1:
        bytes_of(pad.at[1, :, 0:(G - 1) * R], own_s.at[0], own_s.at[0]).wait_send()
        bytes_of(amps.at[0:G - 1], amp_s.at[0], amp_s.at[0]).wait_send()
        bytes_of(scal.at[0:G - 1], scal_s.at[0], scal_s.at[1]).wait_send()
    pl.when(not_first)(lambda: side_bytes(pad.at[0], 0, False).wait_send())
    pl.when(not_last)(lambda: side_bytes(pad.at[0], 0, True).wait_send())
    edges_sent(acc, edge, 2)
    light_red.finish()
    grad_red.finish()
    spread.finish()
    for ch in range(2):
        new_probe[ch] = full[:, :, :, ch].reshape(W, W)
    spread.drain()


def put(obj, probe, obj_out, probe_out, sems):
    copies = [pltpu.make_async_copy(obj, obj_out, sems.at[0]),
              pltpu.make_async_copy(probe, probe_out, sems.at[1])]
    for copy in copies:
        copy.start()
    for copy in copies:
        copy.wait()


def local(T, G, object_field, probe_field, amplitudes, row_start, column_start, live_slots):
    R, B = object_field.shape[1:]
    W = probe_field.shape[1]
    rows = R * G
    p = Plan(T, G, W)
    tables = dft_tables(W)
    spare, blocks = rows - W, W // B
    dma = lambda n: pltpu.SemaphoreType.DMA((max(n, 1),))
    vm = lambda *shape: pltpu.VMEM(shape, F32)

    vmem_limit = 67043328 - 4 * (object_field.size + probe_field.size) - 65536
    smem = pl.BlockSpec(memory_space=pltpu.SMEM)
    hbm = pl.BlockSpec(memory_space=pltpu.HBM)
    vmem = pl.BlockSpec(memory_space=pltpu.VMEM)
    new_obj, new_probe = pl.pallas_call(
        functools.partial(body, T, G),
        out_shape=(pltpu.VMEM(object_field.shape, F32), pltpu.VMEM(probe_field.shape, F32)),
        in_specs=[smem] * 3 + [hbm] * 4,
        out_specs=(vmem, vmem),
        scratch_shapes=[
            pltpu.VMEM((8, 128), jnp.int32),
            pltpu.VMEM((G, 8, 128), jnp.int32),
            vm(2, W, W),
            pltpu.VMEM(tables.shape, BF16),
            dma(4),
            vm(3, 2, rows, B),
            vm(blocks, W, B), vm(G, W, W), vm(G, 2, W, W),
            vm(2, blocks, W + 2 * spare, B), vm(blocks, W + 2 * spare, B),
            vm(3, 2, R, B), vm(3, R, B), vm(2, 2, R, B), vm(2, R, B),
            vm(W, W), vm(8, W), vm(p.part + 8, W),
            vm(p.owners, p.chunk + 8, W), vm(p.H - 1, p.chunk + 8, W),
            vm(2, W, W), vm(2, p.part, W),
            vm(p.owners, 2, p.chunk, W), vm(p.H - 1, 2, p.chunk, W),
            vm(2, p.gs, p.owners, 2, p.chunk, W),
            pltpu.SemaphoreType.REGULAR((max((p.H - 2).bit_length(), 1),)),
            dma(1), dma(4 * G - 4), dma(2), dma(4), dma(1), dma(G - 1), dma(2), dma(2), dma(4),
            dma(2), dma(2), dma(2), dma(2), dma(3), dma(p.owners), dma((p.gs - 1) * p.owners), dma(1),
        ],
        compiler_params=pltpu.CompilerParams(
            collective_id=0, has_side_effects=True, vmem_limit_bytes=vmem_limit),
    )(row_start, column_start, live_slots, object_field, probe_field, amplitudes, tables)
    anywhere = pl.BlockSpec(memory_space=pl.ANY)
    return pl.pallas_call(
        put,
        out_shape=(jax.ShapeDtypeStruct(object_field.shape, F32),
                   jax.ShapeDtypeStruct(probe_field.shape, F32)),
        in_specs=[vmem] * 2,
        out_specs=(anywhere, anywhere),
        scratch_shapes=[dma(2)],
        compiler_params=pltpu.CompilerParams(vmem_limit_bytes=1024 * 1024),
    )(new_obj, new_probe)


def solution(mesh):
    return jax.shard_map(
        functools.partial(local, mesh.shape["tile"], mesh.shape["group"]),
        mesh=mesh,
        in_specs=(
            P(None, "group", "tile"),
            P(),
            P(("tile", "group"), None, None),
            P(("tile", "group")),
            P(("tile", "group")),
            P(("tile", "group")),
        ),
        out_specs=(P(None, "group", "tile"), P()),
        check_vma=False,
    )
```

```python
import functools
import math

import jax
import jax.numpy as jnp
import numpy as np
from jax import lax
from jax.experimental import pallas as pl
from jax.experimental.pallas import tpu as pltpu
from jax.sharding import PartitionSpec as P

MESH = pl.DeviceIdType.MESH
F32 = jnp.float32
BF16 = jnp.bfloat16


def dft_tables(length):
    k = np.arange(length // 2)
    even = (2 * np.outer(k, k)) % length
    odd = np.outer(2 * k + 1, k) % length
    tables = []
    for turns in (even, odd):
        angles = 2.0 * math.pi / length * turns
        cos, sin = np.cos(angles) / math.sqrt(length), np.sin(angles) / math.sqrt(length)
        full = np.block([[cos, sin], [-sin, cos]])
        tables += [full, full.T]
    full = np.stack(tables).astype(np.float32)
    head = full.astype(BF16)
    tail = (full - head.astype(np.float32)).astype(BF16)
    return np.stack([head, tail], axis=1)


EVEN, EVEN_T, ODD, ODD_T = range(4)


def split(x):
    head = x.astype(BF16)
    return head, (x - head.astype(F32)).astype(BF16)


def mm(a, b):
    return jnp.dot(a, b, preferred_element_type=F32)


def cat(parts, axis):
    return jnp.concatenate(parts, axis=axis)


def table_left(table, x):
    head, tail = split(x)
    return mm(cat([table[0], table[0], table[1]], 1), cat([head, tail, head], 0))


def table_right(x, table):
    head, tail = split(x)
    return mm(cat([head, tail, head], 1), cat([table[0], table[0], table[1]], 0))


def fold_in(exits, tables):
    n = exits[0][0].shape[0] // 2
    halves = []
    for sign, table in ((1, tables[EVEN]), (-1, tables[ODD])):
        halves.append(table_left(table, cat(
            [cat([x[:n] + sign * x[n:] for x in parts], 0) for parts in exits], 1)))

    def sides(sign):
        rows = []
        for i in range(len(exits)):
            for y in halves:
                y = y[:, 2 * n * i:2 * n * (i + 1)]
                rows.append(cat([part[:, :n] + sign * part[:, n:] for part in (y[:n], y[n:])], 1))
        return cat(rows, 0)

    return table_right(sides(1), tables[EVEN_T]), table_right(sides(-1), tables[ODD_T])


def fold_out(even, odd, tables):
    n = even.shape[1] // 2
    e, o = table_right(even, tables[EVEN]), table_right(odd, tables[ODD])
    plus, minus = e + o, e - o
    count = even.shape[0] // (2 * n)
    halves = []
    for q, table in ((0, tables[EVEN_T]), (1, tables[ODD_T])):
        parts = []
        for i in range(count):
            r = slice((2 * i + q) * n, (2 * i + q + 1) * n)
            parts.append(cat([cat([plus[r, :n], minus[r, :n]], 1), cat([plus[r, n:], minus[r, n:]], 1)], 0))
        halves.append(table_left(table, cat(parts, 1)))
    plus, minus = halves[0] + halves[1], halves[0] - halves[1]
    return [tuple(cat([side[part, 2 * n * i:2 * n * (i + 1)] for side in (plus, minus)], 0)
                  for part in (slice(0, n), slice(n, 2 * n))) for i in range(count)]


def remote(src, dst, send, recv, tile, group):
    return pltpu.make_async_remote_copy(
        src_ref=src, dst_ref=dst, send_sem=send, recv_sem=recv,
        device_id={"tile": tile, "group": group}, device_id_type=MESH,
    )


class Plan:
    def __init__(self, T, G, W):
        self.H = T // 2
        self.owners = self.H // 2 if self.H % 4 == 0 else self.H
        self.first = (self.H - self.owners) // 2
        self.gs = max(n for n in range(1, G + 1) if G % n == 0 and n * self.owners * 8 <= W // 2)
        self.W, self.half = W, W // 2
        self.part = self.half // self.gs
        self.chunk = self.part // self.owners

    def here(self, t, g):
        self.t, self.g = t, g
        self.k, self.h = lax.div(t, 2), lax.rem(t, 2)
        self.partner = t + 1 - 2 * self.h
        self.s = lax.rem(g, self.gs)
        self.mine = self.k - self.first
        self.low = self.k < self.H // 2
        self.owner = jnp.logical_and(self.mine >= 0, self.mine < self.owners)

    def rows(self, h, s):
        return pl.ds(pl.multiple_of(h * self.half + s * self.part, 8), self.part)

    def chunk_rows(self, h, s, j):
        return pl.ds(pl.multiple_of(h * self.half + s * self.part + j * self.chunk, 8), self.chunk)

    def far_owner(self, i):
        return lax.rem(i + jnp.where(self.low, self.owners // 2, 0), self.owners)

    def near_owner(self, i):
        return jnp.where(self.low, i, self.owners - 1 - i)

    def far_chip(self, i):
        return jnp.where(self.low, self.H - 1 - i, i)


class Reduce:
    def __init__(self, plan, mine, came, sems):
        self.p, self.mine, self.came, self.sems = plan, mine, came, sems

    def copy(self, j):
        p = self.p
        to = p.first + j
        slot = lax.rem(p.k - to + p.H, p.H) - 1
        return remote(self.mine.at[j], self.came.at[slot], self.sems.at[0], self.sems.at[1],
                      2 * to + p.h, p.g)

    def bytes_of(self, ref):
        return remote(ref, ref, self.sems.at[0], self.sems.at[1], self.p.partner, self.p.g)

    def start(self):
        p = self.p
        for i in range(p.owners):
            j = p.far_owner(i)
            pl.when(p.mine != j)(lambda: self.copy(j).start())

    def total(self):
        self.bytes_of(self.came).wait_recv()
        total = self.mine[self.p.mine]
        for slot in range(self.p.H - 1):
            total = total + self.came[slot]
        return total

    def finish(self):
        p = self.p
        pl.when(p.owner)(lambda: self.bytes_of(self.mine.at[0:p.owners - 1]).wait_send())
        pl.when(jnp.logical_not(p.owner))(lambda: self.bytes_of(self.mine).wait_send())


class Gather:
    def __init__(self, plan, full, spare, sent, line, group, relay):
        self.p, self.full, self.spare, self.sent = plan, full, spare, sent
        self.line, self.group, self.relay = line, group, relay

    def slot(self, h, s, j):
        return self.full.at[h, s, j]

    def line_copy(self, chip):
        p = self.p
        slot = self.slot(p.h, p.s, p.mine)
        return remote(slot, slot, self.sent.at[0], self.line.at[p.mine], 2 * chip + p.h, p.g)

    def line_arrival(self, j):
        p = self.p
        slot = self.slot(p.h, p.s, j)
        return remote(slot, slot, self.sent.at[0], self.line.at[j], p.partner, p.g)

    def group_copy(self, d, j, arriving):
        p = self.p
        n = (d - 1) * p.owners + j
        s = lax.rem(p.s + (p.gs - d if arriving else d), p.gs)
        slot = self.slot(p.h, s if arriving else p.s, j)
        return remote(slot, slot, self.sent.at[1], self.group.at[n], p.t, p.g - p.s + s)

    def relay_copy(self, d, j):
        p = self.p
        slot = self.slot(p.h, lax.rem(p.s + p.gs - d, p.gs), j)
        return remote(slot, slot, self.sent.at[2], self.relay.at[0], p.partner, p.g)

    def bytes_of(self, ref, n):
        return remote(ref, ref, self.sent.at[n], self.relay.at[0], self.p.partner, self.p.g)

    def hand_on(self, j):
        for d in range(1, self.p.gs):
            self.group_copy(d, j, False).start()
        self.relay_copy(0, j).start()

    def start(self):
        p = self.p
        self.hand_on(p.mine)
        for i in range(p.H):
            chip = p.far_chip(i)
            pl.when(p.k != chip)(lambda: self.line_copy(chip).start())

    def forward(self):
        p = self.p
        for i in range(p.owners):
            j = p.near_owner(i)

            @pl.when(p.mine != j)
            def _():
                self.line_arrival(j).wait_recv()
                self.hand_on(j)
        for i in range(p.owners):
            for d in range(1, p.gs):
                j = p.near_owner(i)
                self.group_copy(d, j, True).wait_recv()
                self.relay_copy(d, j).start()

    def finish(self):
        self.bytes_of(self.full.at[1 - self.p.h], 2).wait_recv()

    def drain(self):
        p = self.p
        pl.when(p.owner)(lambda: self.bytes_of(self.spare, 0).wait_send())
        if p.gs > 1:
            self.bytes_of(self.full.at[0, 0:p.gs - 1], 1).wait_send()
        self.bytes_of(self.full.at[0], 2).wait_send()


def body(T, G, row_in, column_in, live_in, obj, probe_in, amp, tables_in, new_obj, new_probe,
         scal_in, scal, probe, tables, load_sem, pad, amp_raw, amps, win, freq, terms, light_terms, acc,
         acc_light, edge, edge_light, light_full, light_whole, light_pair, light_mine, light_came,
         grad, grad_pair, grad_mine, grad_came, full, reach, own_s, own_r, side_s, side_r, amp_s,
         amp_r, scal_s, edge_s, edge_r, pair_s, pair_r, light_s, grad_s, sent, line_r, group_r,
         relay_r):
    t, g = lax.axis_index("tile"), lax.axis_index("group")
    R, B = obj.shape[1:]
    W = probe.shape[1]
    rows = pad.shape[2]
    spare, blocks = rows - W, W // B
    p = Plan(T, G, W)
    p.here(t, g)
    not_first, not_last = t > 0, t < T - 1

    def span(group):
        return pl.ds(pl.multiple_of(group * R, 8), R)

    own = pad.at[1, :, span(g)]
    loads = [pltpu.make_async_copy(src, dst, load_sem.at[i]) for i, (src, dst) in enumerate(
        [(obj, own), (probe_in, probe), (tables_in, tables)])]
    amp_loads = [pltpu.make_async_copy(amp.at[0, :, b * B:(b + 1) * B], amp_raw.at[b], load_sem.at[3])
                 for b in range(blocks)]
    for load in amp_loads + loads:
        load.start()

    barrier = pltpu.get_barrier_semaphore()
    count = G - 1
    for j in range(1, G):
        pl.semaphore_signal(barrier, inc=1, device_id={"tile": t, "group": lax.rem(g + j, G)},
                            device_id_type=MESH)
    for d in (-1, 1, -2, 2):
        there = jnp.logical_and(t + d >= 0, t + d < T)

        @pl.when(there)
        def _():
            pl.semaphore_signal(barrier, inc=1, device_id={"tile": t + d, "group": g},
                                device_id_type=MESH)
        count = count + there.astype(jnp.int32)
    line = lax.broadcasted_iota(jnp.int32, scal_in.shape, 0)
    scal_in[...] = jnp.where(line == 0, row_in[0], jnp.where(line == 1, column_in[0], live_in[0]))
    pl.semaphore_wait(barrier, count)

    cut_row = R // 16 * 8
    pieces = [(0, cut_row), (cut_row, R - cut_row)] if cut_row else [(0, R)]

    def piece(group, q):
        return pl.ds(pl.multiple_of(group * R + pieces[q][0], 8), pieces[q][1])

    def to_peer(j, ch, q, arriving):
        peer = lax.rem(g + (G - j if arriving else j), G)
        slot = pad.at[1, ch, piece(peer if arriving else g, q)]
        n = (2 * (j - 1) + ch) * len(pieces) + q
        src = slot if arriving else obj.at[ch, pieces[q][0]:pieces[q][0] + pieces[q][1]]
        return remote(src, slot, own_s.at[0], own_r.at[n], t, peer)

    def to_side(ch, right, src, rows_of):
        dst = pad.at[0 if right else 2, ch, rows_of]
        return remote(src, dst, side_s.at[int(right)], side_r.at[2 * ch + int(right)],
                      t + 1 if right else t - 1, g)

    def side_bytes(ref, ch, right):
        return remote(ref, ref, side_s.at[int(right)], side_r.at[2 * ch + int(right)], p.partner, g)

    def amp_copy(j, arriving):
        peer = lax.rem(g + (G - j if arriving else j), G)
        slot = amps.at[peer if arriving else g]
        return remote(slot, slot, amp_s.at[0], amp_r.at[j - 1], t, peer)

    def scal_copy(j):
        return remote(scal_in, scal.at[g], scal_s.at[0], scal_s.at[1], t, lax.rem(g + j, G))

    def bytes_of(ref, send, recv):
        return remote(ref, ref, send, recv, p.partner, g)

    def edge_copy(src, dst, right, base, arriving):
        n = base + int(right)
        side = dst.at[0 if right else 1]
        if arriving:
            return remote(side, side, edge_s.at[int(right)], edge_r.at[n], t - 1 if right else t + 1, g)
        return remote(src.at[2 if right else 0], side, edge_s.at[int(right)], edge_r.at[n],
                      t + 1 if right else t - 1, g)

    def edges_sent(src, dst, base):
        pl.when(not_first)(lambda: edge_copy(src, dst, False, base, False).wait_send())
        pl.when(not_last)(lambda: edge_copy(src, dst, True, base, False).wait_send())

    def pair_copy(src, dst, n):
        return remote(src, dst, pair_s.at[n], pair_r.at[n], p.partner, g)

    def to_sides(ch, src, rows_of):
        pl.when(not_first)(lambda: to_side(ch, False, src, rows_of).start())
        pl.when(not_last)(lambda: to_side(ch, True, src, rows_of).start())

    for ch in range(2):
        for q in range(len(pieces)):
            for j in range(1, G):
                to_peer(j, ch, q, False).start()
        to_sides(ch, obj.at[ch], span(g))
    for j in range(1, G):
        scal_copy(j).start()

    known, rounds = 1, []
    while known < p.H - 1:
        rounds.append(known)
        known *= 2

    def ends(d):
        return [(p.k - d, p.k >= d), (p.k + d, p.k + d < p.H)]

    def tell(i):
        for chip, there in ends(rounds[i]):
            @pl.when(there)
            def _():
                pl.semaphore_signal(reach.at[i], inc=1,
                                    device_id={"tile": 2 * chip + p.h, "group": g}, device_id_type=MESH)

    def hear(i):
        (_, below), (_, above) = ends(rounds[i])
        pl.semaphore_wait(reach.at[i], below.astype(jnp.int32) + above.astype(jnp.int32))

    tell(0)
    scal[g] = scal_in[...]

    pltpu.make_async_copy(amp_raw, amp_raw, load_sem.at[3]).wait()
    n = W // 2
    a = cat([cat([amp_raw[b, pl.ds(q, n, stride=2), :] for q in range(2)], 0) for b in range(blocks)], 1)
    at = lax.broadcasted_iota(jnp.int32, (W, W), 1)
    at = jnp.where(at < n, 2 * at, 2 * at - (W - 1))
    order = jnp.where(lax.broadcasted_iota(jnp.int32, (W, W), 0) == at, 1.0, 0.0).astype(BF16)
    top = a.astype(BF16)
    rest = a - top.astype(F32)
    middle, low = split(rest)
    amps[g] = mm(top, order) + (mm(middle, order) + mm(low, order))
    for j in range(1, G):
        amp_copy(j, False).start()

    @pl.when(t == 0)
    def _():
        pad[0] = jnp.zeros(pad.shape[1:], F32)
        edge[0] = jnp.zeros(edge.shape[1:], F32)
        edge_light[0] = jnp.zeros(edge_light.shape[1:], F32)

    @pl.when(t == T - 1)
    def _():
        pad[2] = jnp.zeros(pad.shape[1:], F32)
        edge[1] = jnp.zeros(edge.shape[1:], F32)
        edge_light[1] = jnp.zeros(edge_light.shape[1:], F32)

    terms[:, :, :, 0:spare] = jnp.zeros((2, 2, blocks, spare, B), F32)
    terms[:, :, :, spare + W:] = jnp.zeros((2, 2, blocks, spare, B), F32)
    light_terms[:, 0:spare] = jnp.zeros((blocks, spare, B), F32)
    light_terms[:, spare + W:] = jnp.zeros((blocks, spare, B), F32)

    def hold(ref, value):
        for b in range(blocks):
            ref[b, spare:spare + W] = value[:, b * B:(b + 1) * B]

    for load in loads:
        load.wait()
    probe_light = probe[0] * probe[0] + probe[1] * probe[1]
    hold(light_terms, probe_light)
    light_max = jnp.max(probe_light) + 1e-06

    for ch in range(2):
        for q in range(len(pieces)):
            for j in range(1, G):
                to_peer(j, ch, q, True).wait_recv()
                rows_of = piece(lax.rem(g + G - j, G), q)
                to_sides(ch, pad.at[1, ch, rows_of], rows_of)
    if G > 1:
        bytes_of(scal.at[0:G - 1], scal_s.at[0], scal_s.at[1]).wait_recv()

    def next_round(i):
        hear(i)
        if i + 1 < len(rounds):
            tell(i + 1)

    def numbers(k):
        return scal[k, 0, 0], scal[k, 1, 0], scal[k, 2, 0].astype(F32)

    lane = lax.broadcasted_iota(jnp.int32, (8, B), 1)[0:1]

    def placed(ref, row, column):
        first = g * R + spare - row
        shift = lax.rem(column, B)
        stay = lane >= column
        pieces = [pltpu.roll(ref[b, pl.ds(first, R), :], shift, 1) for b in range(blocks)]
        out = [jnp.where(stay, pieces[0], 0.0)]
        out += [jnp.where(stay, pieces[b], pieces[b - 1]) for b in range(1, blocks)]
        return out + [jnp.where(stay, 0.0, pieces[-1])]

    def cut(k, ch):
        row, column, _ = numbers(k)
        shift = lax.rem(B - lax.rem(column, B), B)
        stay = lane < B - column
        pieces = [pltpu.roll(pad[b, ch, pl.ds(row, W), :], shift, 1) for b in range(blocks + 1)]
        for b in range(blocks):
            win[k, ch, :, b * B:(b + 1) * B] = jnp.where(stay, pieces[b], pieces[b + 1])

    def place_light(k, first):
        row, column, weight = numbers(k)
        for b, piece in enumerate(placed(light_terms, row, column)):
            piece = weight * piece
            acc_light[b] = piece if first else acc_light[b] + piece

    def look(k, first):
        weight = numbers(k)[2]
        light = weight * (win[k, 0] * win[k, 0] + win[k, 1] * win[k, 1])
        light_full[...] = light if first else light_full[...] + light

    def ahead(ks):
        pr, pi = probe[0], probe[1]
        exits = []
        for k in ks:
            wr, wi = win[k, 0], win[k, 1]
            exits.append((pr * wr - pi * wi, pr * wi + pi * wr))
        for q, value in enumerate(fold_in(exits, tables)):
            freq[q, 0:len(ks) * W] = value

    def behind(ks, first):
        scaled = []
        for q in range(2):
            rows = []
            for i, k in enumerate(ks):
                value = freq[q, i * W:(i + 1) * W]
                fr, fi = value[:, :n], value[:, n:]
                weight = numbers(k)[2]
                factor = weight - (weight * amps[k, :, q * n:(q + 1) * n]) * lax.rsqrt(
                    jnp.maximum(fr * fr + fi * fi, 0.0625))
                rows.append(cat([fr * factor, fi * factor], 1))
            scaled.append(cat(rows, 0))
        total = None
        for i, (k, (mr, mi)) in enumerate(zip(ks, fold_out(*scaled, tables))):
            wr, wi = win[k, 0], win[k, 1]
            pr, pi = probe[0], probe[1]
            both = (wr * mr + wi * mi, wr * mi - wi * mr)
            total = both if total is None else [a + b for a, b in zip(total, both)]
            hold(terms.at[i, 0], pr * mr + pi * mi)
            hold(terms.at[i, 1], pr * mi - pi * mr)
        for ch in range(2):
            grad[ch] = total[ch] if first else grad[ch] + total[ch]

    def add_terms(ks, first):
        for ch in range(2):
            pieces = [placed(terms.at[i, ch], *numbers(k)[:2]) for i, k in enumerate(ks)]
            for b in range(3):
                piece = sum(p[b] for p in pieces[1:]) + pieces[0][b] if len(ks) > 1 else pieces[0][b]
                acc[b, ch] = piece if first else acc[b, ch] + piece

    def peers(f):
        if G == 2:
            f(1)
        elif G > 2:
            pl.loop(1, G)(f)

    place_light(g, True)
    peers(lambda j: place_light(lax.rem(g + G - j, G), False))
    next_round(0)
    for ch in range(2):
        pl.when(not_last)(lambda: side_bytes(pad.at[2, ch], ch, False).wait_recv())
        pl.when(not_first)(lambda: side_bytes(pad.at[0, ch], ch, True).wait_recv())
    for ch in range(2):
        cut(g, ch)
        peers(lambda j: cut(lax.rem(g + G - j, G), ch))
    look(g, True)
    peers(lambda j: look(lax.rem(g + G - j, G), False))
    light_whole[...] = jnp.sum(light_full[...].reshape(W // 8, 8, W), axis=0)
    pair_copy(light_full.at[p.rows(1 - p.h, p.s)], light_pair.at[0:p.part], 0).start()
    pair_copy(light_whole, light_pair.at[p.part:p.part + 8], 0).start()
    pl.when(not_first)(lambda: edge_copy(acc_light, edge_light, False, 0, False).start())
    pl.when(not_last)(lambda: edge_copy(acc_light, edge_light, True, 0, False).start())
    if len(rounds) > 1:
        next_round(1)

    chosen = (g, 1 - g) if G == 2 else (g,)
    ahead(chosen)
    for i in range(2, len(rounds)):
        next_round(i)
    pair_copy(light_pair, light_pair, 0).wait()
    whole = light_whole[...] + light_pair[p.part:, :]
    for j in range(p.owners):
        light_mine[j, 0:p.chunk] = (light_full[p.chunk_rows(p.h, p.s, j), :]
                                    + light_pair[j * p.chunk:(j + 1) * p.chunk, :])
        light_mine[j, p.chunk:] = whole
    light_red = Reduce(p, light_mine, light_came, light_s)
    light_red.start()

    if G == 2:
        amp_copy(1, True).wait_recv()
    behind(chosen, True)
    if G > 2:
        add_terms(chosen, True)

        def peer_position(j):
            amp_copy(j, True).wait_recv()
            k = lax.rem(g + G - j, G)
            ahead((k,))
            behind((k,), False)
            add_terms((k,), False)

        peers(peer_position)
    grad_pairs = pair_copy(grad.at[:, p.rows(1 - p.h, p.s)], grad_pair, 1)
    grad_pairs.start()
    if G <= 2:
        add_terms(chosen, True)
    grad_pairs.wait()
    for j in range(p.owners):
        grad_mine[j] = (grad[:, p.chunk_rows(p.h, p.s, j), :]
                        + grad_pair[:, j * p.chunk:(j + 1) * p.chunk, :])
    grad_red = Reduce(p, grad_mine, grad_came, grad_s)
    grad_red.start()
    edges_sent(acc_light, edge_light, 0)
    pl.when(not_first)(lambda: edge_copy(acc, edge, False, 2, False).start())
    pl.when(not_last)(lambda: edge_copy(acc, edge, True, 2, False).start())

    spread = Gather(p, full, grad_came, sent, line_r, group_r, relay_r)

    @pl.when(p.owner)
    def _():
        light = light_red.total()
        mean = jnp.sum(light[p.chunk:]) * (1.0 / (W * W))
        below = 1.0 / (light[:p.chunk] + 0.25 * mean + 1e-05)
        here = p.chunk_rows(p.h, p.s, p.mine)
        total = grad_red.total()
        for ch in range(2):
            full[p.h, p.s, p.mine, ch] = probe[ch, here, :] - total[ch] * below
        spread.start()

    spread.forward()
    for src, dst, base in ((acc_light, edge_light, 0), (acc, edge, 2)):
        pl.when(not_last)(lambda: edge_copy(src, dst, False, base, True).wait_recv())
        pl.when(not_first)(lambda: edge_copy(src, dst, True, base, True).wait_recv())
    below = 1.0 / (acc_light[1] + edge_light[0] + edge_light[1] + 0.25 * light_max)
    for ch in range(2):
        new_obj[ch] = own[ch] - (acc[1, ch] + edge[0, ch] + edge[1, ch]) * below

    if G > 1:
        bytes_of(pad.at[1, :, 0:(G - 1) * R], own_s.at[0], own_s.at[0]).wait_send()
        bytes_of(amps.at[0:G - 1], amp_s.at[0], amp_s.at[0]).wait_send()
        bytes_of(scal.at[0:G - 1], scal_s.at[0], scal_s.at[1]).wait_send()
    pl.when(not_first)(lambda: side_bytes(pad.at[0], 0, False).wait_send())
    pl.when(not_last)(lambda: side_bytes(pad.at[0], 0, True).wait_send())
    edges_sent(acc, edge, 2)
    light_red.finish()
    grad_red.finish()
    spread.finish()
    for ch in range(2):
        new_probe[ch] = full[:, :, :, ch].reshape(W, W)
    spread.drain()


def put(obj, probe, obj_out, probe_out, sems):
    copies = [pltpu.make_async_copy(obj, obj_out, sems.at[0]),
              pltpu.make_async_copy(probe, probe_out, sems.at[1])]
    for copy in copies:
        copy.start()
    for copy in copies:
        copy.wait()


def local(T, G, object_field, probe_field, amplitudes, row_start, column_start, live_slots):
    R, B = object_field.shape[1:]
    W = probe_field.shape[1]
    rows = R * G
    p = Plan(T, G, W)
    tables = dft_tables(W)
    spare, blocks = rows - W, W // B
    dma = lambda n: pltpu.SemaphoreType.DMA((max(n, 1),))
    vm = lambda *shape: pltpu.VMEM(shape, F32)

    vmem_limit = 67043328 - 4 * (object_field.size + probe_field.size) - 65536
    smem = pl.BlockSpec(memory_space=pltpu.SMEM)
    hbm = pl.BlockSpec(memory_space=pltpu.HBM)
    vmem = pl.BlockSpec(memory_space=pltpu.VMEM)
    new_obj, new_probe = pl.pallas_call(
        functools.partial(body, T, G),
        out_shape=(pltpu.VMEM(object_field.shape, F32), pltpu.VMEM(probe_field.shape, F32)),
        in_specs=[smem] * 3 + [hbm] * 4,
        out_specs=(vmem, vmem),
        scratch_shapes=[
            pltpu.VMEM((8, 128), jnp.int32),
            pltpu.VMEM((G, 8, 128), jnp.int32),
            vm(2, W, W),
            pltpu.VMEM(tables.shape, BF16),
            dma(4),
            vm(3, 2, rows, B),
            vm(blocks, W, B), vm(G, W, W), vm(G, 2, W, W),
            vm(2, 2 * W, W), vm(2, 2, blocks, W + 2 * spare, B), vm(blocks, W + 2 * spare, B),
            vm(3, 2, R, B), vm(3, R, B), vm(2, 2, R, B), vm(2, R, B),
            vm(W, W), vm(8, W), vm(p.part + 8, W),
            vm(p.owners, p.chunk + 8, W), vm(p.H - 1, p.chunk + 8, W),
            vm(2, W, W), vm(2, p.part, W),
            vm(p.owners, 2, p.chunk, W), vm(p.H - 1, 2, p.chunk, W),
            vm(2, p.gs, p.owners, 2, p.chunk, W),
            pltpu.SemaphoreType.REGULAR((max((p.H - 2).bit_length(), 1),)),
            dma(1), dma(4 * G - 4), dma(2), dma(4), dma(1), dma(G - 1), dma(2), dma(2), dma(4),
            dma(2), dma(2), dma(2), dma(2), dma(3), dma(p.owners), dma((p.gs - 1) * p.owners), dma(1),
        ],
        compiler_params=pltpu.CompilerParams(
            collective_id=0, has_side_effects=True, vmem_limit_bytes=vmem_limit),
    )(row_start, column_start, live_slots, object_field, probe_field, amplitudes, tables)
    anywhere = pl.BlockSpec(memory_space=pl.ANY)
    return pl.pallas_call(
        put,
        out_shape=(jax.ShapeDtypeStruct(object_field.shape, F32),
                   jax.ShapeDtypeStruct(probe_field.shape, F32)),
        in_specs=[vmem] * 2,
        out_specs=(anywhere, anywhere),
        scratch_shapes=[dma(2)],
        compiler_params=pltpu.CompilerParams(vmem_limit_bytes=1024 * 1024),
    )(new_obj, new_probe)


def solution(mesh):
    return jax.shard_map(
        functools.partial(local, mesh.shape["tile"], mesh.shape["group"]),
        mesh=mesh,
        in_specs=(
            P(None, "group", "tile"),
            P(),
            P(("tile", "group"), None, None),
            P(("tile", "group")),
            P(("tile", "group")),
            P(("tile", "group")),
        ),
        out_specs=(P(None, "group", "tile"), P()),
        check_vma=False,
    )
```

```python
import functools
import math

import jax
import jax.numpy as jnp
import numpy as np
from jax import lax
from jax.experimental import pallas as pl
from jax.experimental.pallas import tpu as pltpu
from jax.sharding import PartitionSpec as P

MESH = pl.DeviceIdType.MESH
F32 = jnp.float32
BF16 = jnp.bfloat16


def dft_tables(length):
    k = np.arange(length // 2)
    even = (2 * np.outer(k, k)) % length
    odd = np.outer(2 * k + 1, k) % length
    tables = []
    for turns in (even, odd):
        angles = 2.0 * math.pi / length * turns
        cos, sin = np.cos(angles) / math.sqrt(length), np.sin(angles) / math.sqrt(length)
        full = np.block([[cos, sin], [-sin, cos]])
        tables += [full, full.T]
    full = np.stack(tables).astype(np.float32)
    head = full.astype(BF16)
    tail = (full - head.astype(np.float32)).astype(BF16)
    return np.stack([head, tail], axis=1)


EVEN, EVEN_T, ODD, ODD_T = range(4)


def split(x):
    head = x.astype(BF16)
    return head, (x - head.astype(F32)).astype(BF16)


def mm(a, b):
    return jnp.dot(a, b, preferred_element_type=F32)


def cat(parts, axis):
    return jnp.concatenate(parts, axis=axis)


def table_left(table, x):
    head, tail = split(x)
    return mm(cat([table[0], table[0], table[1]], 1), cat([head, tail, head], 0))


def table_right(x, table):
    head, tail = split(x)
    return mm(cat([head, tail, head], 1), cat([table[0], table[0], table[1]], 0))


def rows_in(exits, tables):
    n = exits[0][0].shape[0] // 2
    return [table_left(table, cat([cat([x[:n] + sign * x[n:] for x in parts], 0) for parts in exits], 1))
            for sign, table in ((1, tables[EVEN]), (-1, tables[ODD]))]


def columns_in(halves, tables):
    n = halves[0].shape[0] // 2

    def sides(sign):
        rows = []
        for i in range(halves[0].shape[1] // (2 * n)):
            for y in halves:
                y = y[:, 2 * n * i:2 * n * (i + 1)]
                rows.append(cat([part[:, :n] + sign * part[:, n:] for part in (y[:n], y[n:])], 1))
        return cat(rows, 0)

    return table_right(sides(1), tables[EVEN_T]), table_right(sides(-1), tables[ODD_T])


def columns_out(even, odd, tables):
    e, o = table_right(even, tables[EVEN]), table_right(odd, tables[ODD])
    return e + o, e - o


def rows_out(side, tables):
    n = side.shape[1] // 2
    halves = []
    for q, table in ((0, tables[EVEN_T]), (1, tables[ODD_T])):
        parts = [side[(2 * i + q) * n:(2 * i + q + 1) * n] for i in range(side.shape[0] // (2 * n))]
        halves.append(table_left(table, cat([cat([x[:, :n], x[:, n:]], 0) for x in parts], 1)))
    plus, minus = halves[0] + halves[1], halves[0] - halves[1]
    return [tuple(cat([x[part, n * i:n * (i + 1)] for x in (plus, minus)], 0)
                  for part in (slice(0, n), slice(n, 2 * n))) for i in range(plus.shape[1] // n)]


def remote(src, dst, send, recv, tile, group):
    return pltpu.make_async_remote_copy(
        src_ref=src, dst_ref=dst, send_sem=send, recv_sem=recv,
        device_id={"tile": tile, "group": group}, device_id_type=MESH,
    )


class Plan:
    def __init__(self, T, G, W):
        self.H = T // 2
        self.owners = self.H // 2 if self.H % 4 == 0 else self.H
        self.first = (self.H - self.owners) // 2
        self.gs = max(n for n in range(1, G + 1) if G % n == 0 and n * self.owners * 8 <= W)
        self.part = W // self.gs
        self.chunk = self.part // self.owners

    def here(self, t, g):
        self.t, self.g = t, g
        self.k, self.h = lax.div(t, 2), lax.rem(t, 2)
        self.partner = t + 1 - 2 * self.h
        self.s = lax.rem(g, self.gs)
        self.mine = self.k - self.first
        self.low = self.k < self.H // 2
        self.owner = jnp.logical_and(self.mine >= 0, self.mine < self.owners)

    def rows(self, s):
        return pl.ds(pl.multiple_of(s * self.part, 8), self.part)

    def chunk_rows(self, s, j):
        return pl.ds(pl.multiple_of(s * self.part + j * self.chunk, 8), self.chunk)

    def far_owner(self, i):
        return lax.rem(i + jnp.where(self.low, self.owners // 2, 0), self.owners)

    def near_owner(self, i):
        return jnp.where(self.low, i, self.owners - 1 - i)

    def far_chip(self, i):
        return jnp.where(self.low, self.H - 1 - i, i)


class Reduce:
    def __init__(self, plan, mine, came, sems):
        self.p, self.mine, self.came, self.sems = plan, mine, came, sems

    def copy(self, j):
        p = self.p
        to = p.first + j
        slot = lax.rem(p.k - to + p.H, p.H) - 1
        return remote(self.mine.at[j], self.came.at[slot], self.sems.at[0], self.sems.at[1],
                      2 * to + p.h, p.g)

    def bytes_of(self, ref):
        return remote(ref, ref, self.sems.at[0], self.sems.at[1], self.p.partner, self.p.g)

    def start(self):
        p = self.p
        for i in range(p.owners):
            j = p.far_owner(i)
            pl.when(p.mine != j)(lambda: self.copy(j).start())

    def total(self):
        self.bytes_of(self.came).wait_recv()
        total = self.mine[self.p.mine]
        for slot in range(self.p.H - 1):
            total = total + self.came[slot]
        return total

    def finish(self):
        p = self.p
        pl.when(p.owner)(lambda: self.bytes_of(self.mine.at[0:p.owners - 1]).wait_send())
        pl.when(jnp.logical_not(p.owner))(lambda: self.bytes_of(self.mine).wait_send())


class Gather:
    def __init__(self, plan, full, spare, sent, line, group, relay):
        self.p, self.full, self.spare, self.sent = plan, full, spare, sent
        self.line, self.group, self.relay = line, group, relay

    def slot(self, h, s, j):
        return self.full.at[h, s, j]

    def line_copy(self, chip):
        p = self.p
        slot = self.slot(p.h, p.s, p.mine)
        return remote(slot, slot, self.sent.at[0], self.line.at[p.mine], 2 * chip + p.h, p.g)

    def line_arrival(self, j):
        p = self.p
        slot = self.slot(p.h, p.s, j)
        return remote(slot, slot, self.sent.at[0], self.line.at[j], p.partner, p.g)

    def group_copy(self, d, j, arriving):
        p = self.p
        n = (d - 1) * p.owners + j
        s = lax.rem(p.s + (p.gs - d if arriving else d), p.gs)
        slot = self.slot(p.h, s if arriving else p.s, j)
        return remote(slot, slot, self.sent.at[1], self.group.at[n], p.t, p.g - p.s + s)

    def relay_copy(self, d, j):
        p = self.p
        slot = self.slot(p.h, lax.rem(p.s + p.gs - d, p.gs), j)
        return remote(slot, slot, self.sent.at[2], self.relay.at[0], p.partner, p.g)

    def bytes_of(self, ref, n):
        return remote(ref, ref, self.sent.at[n], self.relay.at[0], self.p.partner, self.p.g)

    def hand_on(self, j):
        for d in range(1, self.p.gs):
            self.group_copy(d, j, False).start()
        self.relay_copy(0, j).start()

    def start(self):
        p = self.p
        self.hand_on(p.mine)
        for i in range(p.H):
            chip = p.far_chip(i)
            pl.when(p.k != chip)(lambda: self.line_copy(chip).start())

    def forward(self):
        p = self.p
        for i in range(p.owners):
            j = p.near_owner(i)

            @pl.when(p.mine != j)
            def _():
                self.line_arrival(j).wait_recv()
                self.hand_on(j)
        for i in range(p.owners):
            for d in range(1, p.gs):
                j = p.near_owner(i)
                self.group_copy(d, j, True).wait_recv()
                self.relay_copy(d, j).start()

    def finish(self):
        self.bytes_of(self.full.at[1 - self.p.h], 2).wait_recv()

    def drain(self):
        p = self.p
        pl.when(p.owner)(lambda: self.bytes_of(self.spare, 0).wait_send())
        if p.gs > 1:
            self.bytes_of(self.full.at[0, 0:p.gs - 1], 1).wait_send()
        self.bytes_of(self.full.at[0], 2).wait_send()


def body(T, G, row_in, column_in, live_in, obj, probe_in, amp, tables_in, new_obj, new_probe,
         scal_in, scal, probe, tables, load_sem, pad, amp_raw, amps, win, freq, terms, light_terms, acc,
         acc_light, edge, light_full, light_whole, light_pair, light_mine, light_came,
         grad, grad_pair, grad_mine, grad_came, full, reach, own_s, own_r, side_s, side_r, amp_s,
         amp_r, scal_s, edge_s, edge_r, pair_s, pair_r, light_s, grad_s, sent, line_r, group_r,
         relay_r):
    t, g = lax.axis_index("tile"), lax.axis_index("group")
    R, B = obj.shape[1:]
    W = probe.shape[2]
    rows = pad.shape[2]
    spare, blocks = rows - W, W // B
    p = Plan(T, G, W)
    p.here(t, g)
    not_first, not_last = t > 0, t < T - 1

    def span(group):
        return pl.ds(pl.multiple_of(group * R, 8), R)

    own = pad.at[1, :, span(g)]
    loads = [pltpu.make_async_copy(src, dst, load_sem.at[i]) for i, (src, dst) in enumerate(
        [(obj, own), (tables_in, tables)])]
    amp_loads = [pltpu.make_async_copy(amp.at[0, :, b * B:(b + 1) * B], amp_raw.at[b], load_sem.at[3])
                 for b in range(blocks)]
    probe_loads = [pltpu.make_async_copy(probe_in.at[:, :, b * B:(b + 1) * B], probe.at[:, b], load_sem.at[2])
                   for b in range(blocks)]
    for load in amp_loads + probe_loads + loads:
        load.start()

    barrier = pltpu.get_barrier_semaphore()
    count = G - 1
    for j in range(1, G):
        pl.semaphore_signal(barrier, inc=1, device_id={"tile": t, "group": lax.rem(g + j, G)},
                            device_id_type=MESH)
    for d in (-1, 1, -2, 2):
        there = jnp.logical_and(t + d >= 0, t + d < T)

        @pl.when(there)
        def _():
            pl.semaphore_signal(barrier, inc=1, device_id={"tile": t + d, "group": g},
                                device_id_type=MESH)
        count = count + there.astype(jnp.int32)
    line = lax.broadcasted_iota(jnp.int32, scal_in.shape, 0)
    scal_in[...] = jnp.where(line == 0, row_in[0], jnp.where(line == 1, column_in[0], live_in[0]))
    pl.semaphore_wait(barrier, count)

    cut_row = R // 16 * 8
    pieces = [(0, cut_row), (cut_row, R - cut_row)] if cut_row else [(0, R)]

    def piece(group, q):
        return pl.ds(pl.multiple_of(group * R + pieces[q][0], 8), pieces[q][1])

    def to_peer(j, ch, q, arriving):
        peer = lax.rem(g + (G - j if arriving else j), G)
        slot = pad.at[1, ch, piece(peer if arriving else g, q)]
        n = (2 * (j - 1) + ch) * len(pieces) + q
        src = slot if arriving else obj.at[ch, pieces[q][0]:pieces[q][0] + pieces[q][1]]
        return remote(src, slot, own_s.at[0], own_r.at[n], t, peer)

    def to_side(ch, right, src, rows_of):
        dst = pad.at[0 if right else 2, ch, rows_of]
        return remote(src, dst, side_s.at[int(right)], side_r.at[2 * ch + int(right)],
                      t + 1 if right else t - 1, g)

    def side_bytes(ref, ch, right):
        return remote(ref, ref, side_s.at[int(right)], side_r.at[2 * ch + int(right)], p.partner, g)

    def amp_copy(j, arriving):
        peer = lax.rem(g + (G - j if arriving else j), G)
        slot = amps.at[peer if arriving else g]
        return remote(slot, slot, amp_s.at[0], amp_r.at[j - 1], t, peer)

    def scal_copy(j):
        return remote(scal_in, scal.at[1, g], scal_s.at[0], scal_s.at[1], t, lax.rem(g + j, G))

    def scal_side(right):
        return remote(scal.at[1], scal.at[0 if right else 2], scal_s.at[2 + int(right)],
                      scal_s.at[4 + int(right)], t + 1 if right else t - 1, g)

    def bytes_of(ref, send, recv):
        return remote(ref, ref, send, recv, p.partner, g)

    def edge_copy(right):
        return remote(acc.at[2 if right else 0], edge.at[0 if right else 1], edge_s.at[int(right)],
                      edge_r.at[int(right)], t + 1 if right else t - 1, g)

    def pair_copy(src, dst, n):
        return remote(src, dst, pair_s.at[n], pair_r.at[n], p.partner, g)

    def to_sides(ch, src, rows_of):
        pl.when(not_first)(lambda: to_side(ch, False, src, rows_of).start())
        pl.when(not_last)(lambda: to_side(ch, True, src, rows_of).start())

    for j in range(1, G):
        scal_copy(j).start()
    for ch in range(2):
        for q in range(len(pieces)):
            for j in range(1, G):
                to_peer(j, ch, q, False).start()
        to_sides(ch, obj.at[ch], span(g))

    known, rounds = 1, []
    while known < p.H - 1:
        rounds.append(known)
        known *= 2

    def ends(d):
        return [(p.k - d, p.k >= d), (p.k + d, p.k + d < p.H)]

    def tell(i):
        for chip, there in ends(rounds[i]):
            @pl.when(there)
            def _():
                pl.semaphore_signal(reach.at[i], inc=1,
                                    device_id={"tile": 2 * chip + p.h, "group": g}, device_id_type=MESH)

    def hear(i):
        (_, below), (_, above) = ends(rounds[i])
        pl.semaphore_wait(reach.at[i], below.astype(jnp.int32) + above.astype(jnp.int32))

    tell(0)
    scal[1, g] = scal_in[...]

    pltpu.make_async_copy(amp_raw, amp_raw, load_sem.at[3]).wait()
    n = W // 2
    a = cat([cat([amp_raw[b, pl.ds(q, n, stride=2), :] for q in range(2)], 0) for b in range(blocks)], 1)
    at = lax.broadcasted_iota(jnp.int32, (W, W), 1)
    at = jnp.where(at < n, 2 * at, 2 * at - (W - 1))
    order = jnp.where(lax.broadcasted_iota(jnp.int32, (W, W), 0) == at, 1.0, 0.0).astype(BF16)
    top = a.astype(BF16)
    rest = a - top.astype(F32)
    middle, low = split(rest)
    amps[g] = mm(top, order) + (mm(middle, order) + mm(low, order))
    for j in range(1, G):
        amp_copy(j, False).start()

    @pl.when(t == 0)
    def _():
        pad[0] = jnp.zeros(pad.shape[1:], F32)
        edge[0] = jnp.zeros(edge.shape[1:], F32)
        scal[0] = jnp.zeros(scal.shape[1:], jnp.int32)

    @pl.when(t == T - 1)
    def _():
        pad[2] = jnp.zeros(pad.shape[1:], F32)
        edge[1] = jnp.zeros(edge.shape[1:], F32)
        scal[2] = jnp.zeros(scal.shape[1:], jnp.int32)

    terms[:, :, :, 0:spare] = jnp.zeros((2, 2, blocks, spare, B), F32)
    terms[:, :, :, spare + W:] = jnp.zeros((2, 2, blocks, spare, B), F32)
    light_terms[:, 0:spare] = jnp.zeros((blocks, spare, B), F32)
    light_terms[:, spare + W:] = jnp.zeros((blocks, spare, B), F32)

    for load in loads:
        load.wait()
    pltpu.make_async_copy(probe, probe, load_sem.at[2]).wait()
    probe_light = probe[0] * probe[0] + probe[1] * probe[1]
    light_terms[:, spare:spare + W] = probe_light
    light_max = jnp.max(probe_light) + 1e-06

    if G > 1:
        bytes_of(scal.at[1, 0:G - 1], scal_s.at[0], scal_s.at[1]).wait_recv()
    pl.when(not_first)(lambda: scal_side(False).start())
    pl.when(not_last)(lambda: scal_side(True).start())
    for ch in range(2):
        for q in range(len(pieces)):
            for j in range(1, G):
                to_peer(j, ch, q, True).wait_recv()
                rows_of = piece(lax.rem(g + G - j, G), q)
                to_sides(ch, pad.at[1, ch, rows_of], rows_of)

    def next_round(i):
        hear(i)
        if i + 1 < len(rounds):
            tell(i + 1)

    def numbers(k, side=1):
        return scal[side, k, 0, 0], scal[side, k, 1, 0], scal[side, k, 2, 0].astype(F32)

    lane = lax.broadcasted_iota(jnp.int32, (8, B), 1)[0:1]

    def placed(ref, row, column):
        first = g * R + spare - row
        shift = lax.rem(column, B)
        stay = lane >= column
        pieces = [pltpu.roll(ref[b, pl.ds(first, R), :], shift, 1) for b in range(blocks)]
        out = [jnp.where(stay, pieces[0], 0.0)]
        out += [jnp.where(stay, pieces[b], pieces[b - 1]) for b in range(1, blocks)]
        return out + [jnp.where(stay, 0.0, pieces[-1])]

    def cut(k, ch):
        row, column, _ = numbers(k)
        shift = lax.rem(B - lax.rem(column, B), B)
        stay = lane < B - column
        pieces = [pltpu.roll(pad[b, ch, pl.ds(row, W), :], shift, 1) for b in range(blocks + 1)]
        for b in range(blocks):
            win[k, ch, b] = jnp.where(stay, pieces[b], pieces[b + 1])

    def place_light(k):
        total = None
        for side in range(3):
            row, column, weight = numbers(k, side)
            piece = weight * placed(light_terms, row, column)[2 - side]
            total = piece if total is None else total + piece
        acc_light[...] += total

    def look(k, first):
        weight = numbers(k)[2]
        light = weight * (win[k, 0] * win[k, 0] + win[k, 1] * win[k, 1])
        light_full[...] = light if first else light_full[...] + light

    def wide(ref):
        return cat([ref[b] for b in range(blocks)], 1)

    def begin(ks):
        pr, pi = wide(probe.at[0]), wide(probe.at[1])
        exits = []
        for k in ks:
            wr, wi = wide(win.at[k, 0]), wide(win.at[k, 1])
            exits.append((pr * wr - pi * wi, pr * wi + pi * wr))
        return rows_in(exits, tables)

    def ahead(halves, count):
        for q, value in enumerate(columns_in(halves, tables)):
            freq[q, 0:count * W] = value

    def behind(ks):
        scaled = []
        for q in range(2):
            rows = []
            for i, k in enumerate(ks):
                value = freq[q, i * W:(i + 1) * W]
                fr, fi = value[:, :n], value[:, n:]
                weight = numbers(k)[2]
                factor = weight - (weight * amps[k, :, q * n:(q + 1) * n]) * lax.rsqrt(
                    jnp.maximum(fr * fr + fi * fi, 0.0625))
                rows.append(cat([fr * factor, fi * factor], 1))
            scaled.append(cat(rows, 0))
        for c, value in enumerate(columns_out(*scaled, tables)):
            freq[c, 0:len(ks) * W] = value

    def end(ks, c, first):
        total = None
        for i, (k, (mr, mi)) in enumerate(zip(ks, rows_out(freq[c, 0:len(ks) * W], tables))):
            wr, wi = win[k, 0, c], win[k, 1, c]
            pr, pi = probe[0, c], probe[1, c]
            both = (wr * mr + wi * mi, wr * mi - wi * mr)
            total = both if total is None else [a + b for a, b in zip(total, both)]
            terms[i, 0, c, spare:spare + W] = pr * mr + pi * mi
            terms[i, 1, c, spare:spare + W] = pr * mi - pi * mr
        for ch in range(2):
            grad[c, ch] = total[ch] if first else grad[c, ch] + total[ch]

    def add_terms(ks, first):
        for ch in range(2):
            pieces = [placed(terms.at[i, ch], *numbers(k)[:2]) for i, k in enumerate(ks)]
            for b in range(3):
                piece = sum(p[b] for p in pieces[1:]) + pieces[0][b] if len(ks) > 1 else pieces[0][b]
                acc[b, ch] = piece if first else acc[b, ch] + piece

    def peers(f):
        if G == 2:
            f(1)
        elif G > 2:
            pl.loop(1, G)(f)

    pl.when(not_last)(lambda: scal_side(False).wait_recv())
    pl.when(not_first)(lambda: scal_side(True).wait_recv())
    acc_light[...] = jnp.zeros(acc_light.shape, F32)
    if G <= 2:
        for k in range(G):
            place_light(k)
    else:
        pl.loop(0, G)(place_light)
    acc_light[...] = 1.0 / (acc_light[...] + 0.25 * light_max)
    next_round(0)
    for ch in range(2):
        pl.when(not_last)(lambda: side_bytes(pad.at[2, ch], ch, False).wait_recv())
        pl.when(not_first)(lambda: side_bytes(pad.at[0, ch], ch, True).wait_recv())
    if len(rounds) > 1:
        next_round(1)
    for ch in range(2):
        cut(g, ch)
        peers(lambda j: cut(lax.rem(g + G - j, G), ch))
    look(g, True)
    peers(lambda j: look(lax.rem(g + G - j, G), False))
    chosen = (g, 1 - g) if G == 2 else (g,)
    light_whole[...] = jnp.sum(light_full[...].reshape(blocks * W // 8, 8, B), axis=0)
    pair_copy(light_full.at[1 - p.h, p.rows(p.s)], light_pair.at[0:p.part], 0).start()
    pair_copy(light_whole, light_pair.at[p.part:p.part + 8], 0).start()
    ahead(begin(chosen), len(chosen))
    for i in range(2, len(rounds)):
        next_round(i)
    pair_copy(light_pair, light_pair, 0).wait()
    whole = light_whole[...] + light_pair[p.part:, :]
    for j in range(p.owners):
        light_mine[j, 0:p.chunk] = (light_full[p.h, p.chunk_rows(p.s, j), :]
                                    + light_pair[j * p.chunk:(j + 1) * p.chunk, :])
        light_mine[j, p.chunk:] = whole
    light_red = Reduce(p, light_mine, light_came, light_s)
    light_red.start()

    if G == 2:
        amp_copy(1, True).wait_recv()
    behind(chosen)
    if G > 2:
        for c in range(blocks):
            end(chosen, c, True)
        add_terms(chosen, True)

        def peer_position(j):
            amp_copy(j, True).wait_recv()
            k = lax.rem(g + G - j, G)
            ahead(begin((k,)), 1)
            behind((k,))
            for c in range(blocks):
                end((k,), c, False)
            add_terms((k,), False)

        peers(peer_position)
    else:
        end(chosen, 1 - p.h, True)
    grad_pairs = pair_copy(grad.at[1 - p.h, :, p.rows(p.s)], grad_pair, 1)
    grad_pairs.start()
    if G <= 2:
        end(chosen, p.h, True)
        add_terms(chosen, True)
    grad_pairs.wait()
    for j in range(p.owners):
        grad_mine[j] = (grad[p.h, :, p.chunk_rows(p.s, j), :]
                        + grad_pair[:, j * p.chunk:(j + 1) * p.chunk, :])
    grad_red = Reduce(p, grad_mine, grad_came, grad_s)
    grad_red.start()
    pl.when(not_first)(lambda: edge_copy(False).start())
    pl.when(not_last)(lambda: edge_copy(True).start())

    spread = Gather(p, full, grad_came, sent, line_r, group_r, relay_r)

    @pl.when(p.owner)
    def _():
        light = light_red.total()
        mean = jnp.sum(light[p.chunk:]) * (1.0 / (W * W))
        below = 1.0 / (light[:p.chunk] + 0.25 * mean + 1e-05)
        here = p.chunk_rows(p.s, p.mine)
        total = grad_red.total()
        for ch in range(2):
            full[p.h, p.s, p.mine, ch] = probe[ch, p.h, here, :] - total[ch] * below
        spread.start()

    spread.forward()
    pl.when(not_last)(lambda: edge_copy(False).wait_recv())
    pl.when(not_first)(lambda: edge_copy(True).wait_recv())
    for ch in range(2):
        new_obj[ch] = own[ch] - (acc[1, ch] + edge[0, ch] + edge[1, ch]) * acc_light[...]

    if G > 1:
        bytes_of(pad.at[1, :, 0:(G - 1) * R], own_s.at[0], own_s.at[0]).wait_send()
        bytes_of(amps.at[0:G - 1], amp_s.at[0], amp_s.at[0]).wait_send()
        bytes_of(scal.at[1, 0:G - 1], scal_s.at[0], scal_s.at[1]).wait_send()
    pl.when(not_first)(lambda: side_bytes(pad.at[0], 0, False).wait_send())
    pl.when(not_last)(lambda: side_bytes(pad.at[0], 0, True).wait_send())
    for right, there in ((False, not_first), (True, not_last)):
        pl.when(there)(lambda: scal_side(right).wait_send())
        pl.when(there)(lambda: edge_copy(right).wait_send())
    light_red.finish()
    grad_red.finish()
    spread.finish()
    for ch in range(2):
        for b in range(blocks):
            new_probe[ch, :, b * B:(b + 1) * B] = full[b, :, :, ch].reshape(W, B)
    spread.drain()


def put(obj, probe, obj_out, probe_out, sems):
    copies = [pltpu.make_async_copy(obj, obj_out, sems.at[0]),
              pltpu.make_async_copy(probe, probe_out, sems.at[1])]
    for copy in copies:
        copy.start()
    for copy in copies:
        copy.wait()


def local(T, G, object_field, probe_field, amplitudes, row_start, column_start, live_slots):
    R, B = object_field.shape[1:]
    W = probe_field.shape[1]
    rows = R * G
    p = Plan(T, G, W)
    tables = dft_tables(W)
    spare, blocks = rows - W, W // B
    dma = lambda n: pltpu.SemaphoreType.DMA((max(n, 1),))
    vm = lambda *shape: pltpu.VMEM(shape, F32)

    vmem_limit = 67043328 - 4 * (object_field.size + probe_field.size) - 65536
    smem = pl.BlockSpec(memory_space=pltpu.SMEM)
    hbm = pl.BlockSpec(memory_space=pltpu.HBM)
    vmem = pl.BlockSpec(memory_space=pltpu.VMEM)
    new_obj, new_probe = pl.pallas_call(
        functools.partial(body, T, G),
        out_shape=(pltpu.VMEM(object_field.shape, F32), pltpu.VMEM(probe_field.shape, F32)),
        in_specs=[smem] * 3 + [hbm] * 4,
        out_specs=(vmem, vmem),
        scratch_shapes=[
            pltpu.VMEM((8, 128), jnp.int32),
            pltpu.VMEM((3, G, 8, 128), jnp.int32),
            vm(2, blocks, W, B),
            pltpu.VMEM(tables.shape, BF16),
            dma(4),
            vm(3, 2, rows, B),
            vm(blocks, W, B), vm(G, W, W), vm(G, 2, blocks, W, B),
            vm(2, 2 * W, W), vm(2, 2, blocks, W + 2 * spare, B), vm(blocks, W + 2 * spare, B),
            vm(3, 2, R, B), vm(R, B), vm(2, 2, R, B),
            vm(blocks, W, B), vm(8, B), vm(p.part + 8, B),
            vm(p.owners, p.chunk + 8, B), vm(p.H - 1, p.chunk + 8, B),
            vm(blocks, 2, W, B), vm(2, p.part, B),
            vm(p.owners, 2, p.chunk, B), vm(p.H - 1, 2, p.chunk, B),
            vm(2, p.gs, p.owners, 2, p.chunk, B),
            pltpu.SemaphoreType.REGULAR((max((p.H - 2).bit_length(), 1),)),
            dma(1), dma(4 * G - 4), dma(2), dma(4), dma(1), dma(G - 1), dma(6), dma(2), dma(2),
            dma(2), dma(2), dma(2), dma(2), dma(3), dma(p.owners), dma((p.gs - 1) * p.owners), dma(1),
        ],
        compiler_params=pltpu.CompilerParams(
            collective_id=0, has_side_effects=True, vmem_limit_bytes=vmem_limit),
    )(row_start, column_start, live_slots, object_field, probe_field, amplitudes, tables)
    anywhere = pl.BlockSpec(memory_space=pl.ANY)
    return pl.pallas_call(
        put,
        out_shape=(jax.ShapeDtypeStruct(object_field.shape, F32),
                   jax.ShapeDtypeStruct(probe_field.shape, F32)),
        in_specs=[vmem] * 2,
        out_specs=(anywhere, anywhere),
        scratch_shapes=[dma(2)],
        compiler_params=pltpu.CompilerParams(vmem_limit_bytes=1024 * 1024),
    )(new_obj, new_probe)


def solution(mesh):
    return jax.shard_map(
        functools.partial(local, mesh.shape["tile"], mesh.shape["group"]),
        mesh=mesh,
        in_specs=(
            P(None, "group", "tile"),
            P(),
            P(("tile", "group"), None, None),
            P(("tile", "group")),
            P(("tile", "group")),
            P(("tile", "group")),
        ),
        out_specs=(P(None, "group", "tile"), P()),
        check_vma=False,
    )
```

```python
import functools
import math

import jax
import jax.numpy as jnp
import numpy as np
from jax import lax
from jax.experimental import pallas as pl
from jax.experimental.pallas import tpu as pltpu
from jax.sharding import PartitionSpec as P

MESH = pl.DeviceIdType.MESH
F32 = jnp.float32
BF16 = jnp.bfloat16


def dft_tables(length):
    k = np.arange(length // 2)
    even = (2 * np.outer(k, k)) % length
    odd = np.outer(2 * k + 1, k) % length
    tables = []
    for turns in (even, odd):
        angles = 2.0 * math.pi / length * turns
        cos, sin = np.cos(angles) / math.sqrt(length), np.sin(angles) / math.sqrt(length)
        full = np.block([[cos, sin], [-sin, cos]])
        tables += [full, full.T]
    full = np.stack(tables).astype(np.float32)
    head = full.astype(BF16)
    tail = (full - head.astype(np.float32)).astype(BF16)
    return np.stack([head, tail], axis=1)


EVEN, EVEN_T, ODD, ODD_T = range(4)


def split(x):
    head = x.astype(BF16)
    return head, (x - head.astype(F32)).astype(BF16)


def mm(a, b):
    return jnp.dot(a, b, preferred_element_type=F32)


def cat(parts, axis):
    return jnp.concatenate(parts, axis=axis)


def table_left(table, x):
    head, tail = split(x)
    return mm(cat([table[0], table[0], table[1]], 1), cat([head, tail, head], 0))


def table_right(x, table):
    head, tail = split(x)
    return mm(cat([head, tail, head], 1), cat([table[0], table[0], table[1]], 0))


def rows_in(exits, tables):
    n = exits[0][0].shape[0] // 2
    return [table_left(table, cat([cat([x[:n] + sign * x[n:] for x in parts], 0) for parts in exits], 1))
            for sign, table in ((1, tables[EVEN]), (-1, tables[ODD]))]


def columns_in(halves, tables):
    n = halves[0].shape[0] // 2

    def sides(sign):
        rows = []
        for i in range(halves[0].shape[1] // (2 * n)):
            for y in halves:
                y = y[:, 2 * n * i:2 * n * (i + 1)]
                rows.append(cat([part[:, :n] + sign * part[:, n:] for part in (y[:n], y[n:])], 1))
        return cat(rows, 0)

    return table_right(sides(1), tables[EVEN_T]), table_right(sides(-1), tables[ODD_T])


def columns_out(even, odd, tables):
    e, o = table_right(even, tables[EVEN]), table_right(odd, tables[ODD])
    return e + o, e - o


def rows_out(side, tables):
    n = side.shape[1] // 2
    halves = []
    for q, table in ((0, tables[EVEN_T]), (1, tables[ODD_T])):
        parts = [side[(2 * i + q) * n:(2 * i + q + 1) * n] for i in range(side.shape[0] // (2 * n))]
        halves.append(table_left(table, cat([cat([x[:, :n], x[:, n:]], 0) for x in parts], 1)))
    plus, minus = halves[0] + halves[1], halves[0] - halves[1]
    return [tuple(cat([x[part, n * i:n * (i + 1)] for x in (plus, minus)], 0)
                  for part in (slice(0, n), slice(n, 2 * n))) for i in range(plus.shape[1] // n)]


def remote(src, dst, send, recv, tile, group):
    return pltpu.make_async_remote_copy(
        src_ref=src, dst_ref=dst, send_sem=send, recv_sem=recv,
        device_id={"tile": tile, "group": group}, device_id_type=MESH,
    )


class Plan:
    def __init__(self, T, G, W):
        self.H = T // 2
        self.owners = self.H
        self.first = (self.H - self.owners) // 2
        self.gs = max(n for n in range(1, G + 1) if G % n == 0 and n * self.owners * 8 <= W)
        self.part = W // self.gs
        self.chunk = self.part // self.owners

    def here(self, t, g):
        self.t, self.g = t, g
        self.k, self.h = lax.div(t, 2), lax.rem(t, 2)
        self.partner = t + 1 - 2 * self.h
        self.s = lax.rem(g, self.gs)
        self.mine = self.k - self.first
        self.low = self.k < self.H // 2
        self.owner = jnp.logical_and(self.mine >= 0, self.mine < self.owners)

    def rows(self, s):
        return pl.ds(pl.multiple_of(s * self.part, 8), self.part)

    def chunk_rows(self, s, j):
        return pl.ds(pl.multiple_of(s * self.part + j * self.chunk, 8), self.chunk)

    def far_owner(self, i):
        return lax.rem(i + jnp.where(self.low, self.owners // 2, 0), self.owners)

    def near_owner(self, i):
        return jnp.where(self.low, i, self.owners - 1 - i)

    def far_chip(self, i):
        return jnp.where(self.low, self.H - 1 - i, i)


class Reduce:
    def __init__(self, plan, mine, came, sems):
        self.p, self.mine, self.came, self.sems = plan, mine, came, sems

    def copy(self, j):
        p = self.p
        to = p.first + j
        slot = lax.rem(p.k - to + p.H, p.H) - 1
        return remote(self.mine.at[j], self.came.at[slot], self.sems.at[0], self.sems.at[1],
                      2 * to + p.h, p.g)

    def bytes_of(self, ref):
        return remote(ref, ref, self.sems.at[0], self.sems.at[1], self.p.partner, self.p.g)

    def start(self):
        p = self.p
        for i in range(p.owners):
            j = p.far_owner(i)
            pl.when(p.mine != j)(lambda: self.copy(j).start())

    def total(self):
        self.bytes_of(self.came).wait_recv()
        total = self.mine[self.p.mine]
        for slot in range(self.p.H - 1):
            total = total + self.came[slot]
        return total

    def finish(self):
        p = self.p
        self.bytes_of(self.mine.at[0:p.owners - 1]).wait_send()


class Gather:
    def __init__(self, plan, full, spare, sent, line, group, relay):
        self.p, self.full, self.spare, self.sent = plan, full, spare, sent
        self.line, self.group, self.relay = line, group, relay

    def slot(self, h, s, j):
        return self.full.at[h, s, j]

    def line_copy(self, chip):
        p = self.p
        slot = self.slot(p.h, p.s, p.mine)
        return remote(slot, slot, self.sent.at[0], self.line.at[p.mine], 2 * chip + p.h, p.g)

    def line_arrival(self, j):
        p = self.p
        slot = self.slot(p.h, p.s, j)
        return remote(slot, slot, self.sent.at[0], self.line.at[j], p.partner, p.g)

    def group_copy(self, d, j, arriving):
        p = self.p
        n = (d - 1) * p.owners + j
        s = lax.rem(p.s + (p.gs - d if arriving else d), p.gs)
        slot = self.slot(p.h, s if arriving else p.s, j)
        return remote(slot, slot, self.sent.at[1], self.group.at[n], p.t, p.g - p.s + s)

    def relay_copy(self, d, j):
        p = self.p
        slot = self.slot(p.h, lax.rem(p.s + p.gs - d, p.gs), j)
        return remote(slot, slot, self.sent.at[2], self.relay.at[0], p.partner, p.g)

    def bytes_of(self, ref, n):
        return remote(ref, ref, self.sent.at[n], self.relay.at[0], self.p.partner, self.p.g)

    def hand_on(self, j):
        for d in range(1, self.p.gs):
            self.group_copy(d, j, False).start()
        self.relay_copy(0, j).start()

    def start(self):
        p = self.p
        self.hand_on(p.mine)
        for i in range(p.H):
            chip = p.far_chip(i)
            pl.when(p.k != chip)(lambda: self.line_copy(chip).start())

    def forward(self):
        p = self.p
        for i in range(p.owners):
            j = p.near_owner(i)

            @pl.when(p.mine != j)
            def _():
                self.line_arrival(j).wait_recv()
                self.hand_on(j)
        for i in range(p.owners):
            for d in range(1, p.gs):
                j = p.near_owner(i)
                self.group_copy(d, j, True).wait_recv()
                self.relay_copy(d, j).start()

    def finish(self):
        self.bytes_of(self.full.at[1 - self.p.h], 2).wait_recv()

    def drain(self):
        p = self.p
        pl.when(p.owner)(lambda: self.bytes_of(self.spare, 0).wait_send())
        if p.gs > 1:
            self.bytes_of(self.full.at[0, 0:p.gs - 1], 1).wait_send()
        self.bytes_of(self.full.at[0], 2).wait_send()


def body(T, G, row_in, column_in, live_in, obj, probe_in, amp, tables_in, new_obj, new_probe,
         scal_in, scal, probe, tables, load_sem, pad, amp_raw, amps, win, freq, terms, light_terms, acc,
         acc_light, edge, light_full, light_whole, light_pair, light_mine, light_came,
         grad, grad_pair, grad_mine, grad_came, full, reach, own_s, own_r, side_s, side_r, amp_s,
         amp_r, scal_s, edge_s, edge_r, pair_s, pair_r, light_s, grad_s, sent, line_r, group_r,
         relay_r):
    t, g = lax.axis_index("tile"), lax.axis_index("group")
    R, B = obj.shape[1:]
    W = probe.shape[2]
    rows = pad.shape[2]
    spare, blocks = rows - W, W // B
    p = Plan(T, G, W)
    p.here(t, g)
    not_first, not_last = t > 0, t < T - 1

    def span(group):
        return pl.ds(pl.multiple_of(group * R, 8), R)

    own = pad.at[1, :, span(g)]
    loads = [pltpu.make_async_copy(src, dst, load_sem.at[i]) for i, (src, dst) in enumerate(
        [(obj, own), (tables_in, tables)])]
    amp_loads = [pltpu.make_async_copy(amp.at[0, :, b * B:(b + 1) * B], amp_raw.at[b], load_sem.at[3])
                 for b in range(blocks)]
    probe_loads = [pltpu.make_async_copy(probe_in.at[:, :, b * B:(b + 1) * B], probe.at[:, b], load_sem.at[2])
                   for b in range(blocks)]
    for load in amp_loads + probe_loads + loads:
        load.start()

    barrier = pltpu.get_barrier_semaphore()
    count = G - 1
    for j in range(1, G):
        pl.semaphore_signal(barrier, inc=1, device_id={"tile": t, "group": lax.rem(g + j, G)},
                            device_id_type=MESH)
    for d in (-1, 1, -2, 2):
        there = jnp.logical_and(t + d >= 0, t + d < T)

        @pl.when(there)
        def _():
            pl.semaphore_signal(barrier, inc=1, device_id={"tile": t + d, "group": g},
                                device_id_type=MESH)
        count = count + there.astype(jnp.int32)
    line = lax.broadcasted_iota(jnp.int32, scal_in.shape, 0)
    scal_in[...] = jnp.where(line == 0, row_in[0], jnp.where(line == 1, column_in[0], live_in[0]))
    pl.semaphore_wait(barrier, count)

    cut_row = R // 16 * 8
    pieces = [(0, cut_row), (cut_row, R - cut_row)] if cut_row else [(0, R)]

    def piece(group, q):
        return pl.ds(pl.multiple_of(group * R + pieces[q][0], 8), pieces[q][1])

    def to_peer(j, ch, q, arriving):
        peer = lax.rem(g + (G - j if arriving else j), G)
        slot = pad.at[1, ch, piece(peer if arriving else g, q)]
        n = (2 * (j - 1) + ch) * len(pieces) + q
        src = slot if arriving else obj.at[ch, pieces[q][0]:pieces[q][0] + pieces[q][1]]
        return remote(src, slot, own_s.at[0], own_r.at[n], t, peer)

    def to_side(ch, right, src, rows_of):
        dst = pad.at[0 if right else 2, ch, rows_of]
        return remote(src, dst, side_s.at[int(right)], side_r.at[2 * ch + int(right)],
                      t + 1 if right else t - 1, g)

    def side_bytes(ref, ch, right):
        return remote(ref, ref, side_s.at[int(right)], side_r.at[2 * ch + int(right)], p.partner, g)

    def amp_copy(j, arriving):
        peer = lax.rem(g + (G - j if arriving else j), G)
        slot = amps.at[peer if arriving else g]
        return remote(slot, slot, amp_s.at[0], amp_r.at[j - 1], t, peer)

    def scal_copy(j):
        return remote(scal_in, scal.at[1, g], scal_s.at[0], scal_s.at[1], t, lax.rem(g + j, G))

    def scal_side(right):
        return remote(scal.at[1], scal.at[0 if right else 2], scal_s.at[2 + int(right)],
                      scal_s.at[4 + int(right)], t + 1 if right else t - 1, g)

    def bytes_of(ref, send, recv):
        return remote(ref, ref, send, recv, p.partner, g)

    def edge_copy(right):
        return remote(acc.at[2 if right else 0], edge.at[0 if right else 1], edge_s.at[int(right)],
                      edge_r.at[int(right)], t + 1 if right else t - 1, g)

    def pair_copy(src, dst, n):
        return remote(src, dst, pair_s.at[n], pair_r.at[n], p.partner, g)

    def to_sides(ch, src, rows_of):
        pl.when(not_first)(lambda: to_side(ch, False, src, rows_of).start())
        pl.when(not_last)(lambda: to_side(ch, True, src, rows_of).start())

    for j in range(1, G):
        scal_copy(j).start()
    for ch in range(2):
        for q in range(len(pieces)):
            for j in range(1, G):
                to_peer(j, ch, q, False).start()
        to_sides(ch, obj.at[ch], span(g))

    known, rounds = 1, []
    while known < p.H - 1:
        rounds.append(known)
        known *= 2

    def ends(d):
        return [(p.k - d, p.k >= d), (p.k + d, p.k + d < p.H)]

    def tell(i):
        for chip, there in ends(rounds[i]):
            @pl.when(there)
            def _():
                pl.semaphore_signal(reach.at[i], inc=1,
                                    device_id={"tile": 2 * chip + p.h, "group": g}, device_id_type=MESH)

    def hear(i):
        (_, below), (_, above) = ends(rounds[i])
        pl.semaphore_wait(reach.at[i], below.astype(jnp.int32) + above.astype(jnp.int32))

    tell(0)
    scal[1, g] = scal_in[...]

    pltpu.make_async_copy(amp_raw, amp_raw, load_sem.at[3]).wait()
    n = W // 2
    a = cat([cat([amp_raw[b, pl.ds(q, n, stride=2), :] for q in range(2)], 0) for b in range(blocks)], 1)
    at = lax.broadcasted_iota(jnp.int32, (W, W), 1)
    at = jnp.where(at < n, 2 * at, 2 * at - (W - 1))
    order = jnp.where(lax.broadcasted_iota(jnp.int32, (W, W), 0) == at, 1.0, 0.0).astype(BF16)
    top = a.astype(BF16)
    rest = a - top.astype(F32)
    middle, low = split(rest)
    amps[g] = mm(top, order) + (mm(middle, order) + mm(low, order))
    for j in range(1, G):
        amp_copy(j, False).start()

    @pl.when(t == 0)
    def _():
        pad[0] = jnp.zeros(pad.shape[1:], F32)
        edge[0] = jnp.zeros(edge.shape[1:], F32)
        scal[0] = jnp.zeros(scal.shape[1:], jnp.int32)

    @pl.when(t == T - 1)
    def _():
        pad[2] = jnp.zeros(pad.shape[1:], F32)
        edge[1] = jnp.zeros(edge.shape[1:], F32)
        scal[2] = jnp.zeros(scal.shape[1:], jnp.int32)

    terms[:, :, :, 0:spare] = jnp.zeros((2, 2, blocks, spare, B), F32)
    terms[:, :, :, spare + W:] = jnp.zeros((2, 2, blocks, spare, B), F32)
    light_terms[:, 0:spare] = jnp.zeros((blocks, spare, B), F32)
    light_terms[:, spare + W:] = jnp.zeros((blocks, spare, B), F32)

    for load in loads:
        load.wait()
    pltpu.make_async_copy(probe, probe, load_sem.at[2]).wait()
    probe_light = probe[0] * probe[0] + probe[1] * probe[1]
    light_terms[:, spare:spare + W] = probe_light
    light_max = jnp.max(probe_light) + 1e-06

    if G > 1:
        bytes_of(scal.at[1, 0:G - 1], scal_s.at[0], scal_s.at[1]).wait_recv()
    pl.when(not_first)(lambda: scal_side(False).start())
    pl.when(not_last)(lambda: scal_side(True).start())
    for ch in range(2):
        for q in range(len(pieces)):
            for j in range(1, G):
                to_peer(j, ch, q, True).wait_recv()
                rows_of = piece(lax.rem(g + G - j, G), q)
                to_sides(ch, pad.at[1, ch, rows_of], rows_of)

    def next_round(i):
        hear(i)
        if i + 1 < len(rounds):
            tell(i + 1)

    def numbers(k, side=1):
        return scal[side, k, 0, 0], scal[side, k, 1, 0], scal[side, k, 2, 0].astype(F32)

    lane = lax.broadcasted_iota(jnp.int32, (8, B), 1)[0:1]

    def placed(ref, row, column):
        first = g * R + spare - row
        shift = lax.rem(column, B)
        stay = lane >= column
        pieces = [pltpu.roll(ref[b, pl.ds(first, R), :], shift, 1) for b in range(blocks)]
        out = [jnp.where(stay, pieces[0], 0.0)]
        out += [jnp.where(stay, pieces[b], pieces[b - 1]) for b in range(1, blocks)]
        return out + [jnp.where(stay, 0.0, pieces[-1])]

    def cut(k, ch):
        row, column, _ = numbers(k)
        shift = lax.rem(B - lax.rem(column, B), B)
        stay = lane < B - column
        pieces = [pltpu.roll(pad[b, ch, pl.ds(row, W), :], shift, 1) for b in range(blocks + 1)]
        for b in range(blocks):
            win[k, ch, b] = jnp.where(stay, pieces[b], pieces[b + 1])

    def place_light(k):
        total = None
        for side in range(3):
            row, column, weight = numbers(k, side)
            piece = weight * placed(light_terms, row, column)[2 - side]
            total = piece if total is None else total + piece
        acc_light[...] += total

    def look(k, first):
        weight = numbers(k)[2]
        light = weight * (win[k, 0] * win[k, 0] + win[k, 1] * win[k, 1])
        light_full[...] = light if first else light_full[...] + light

    def wide(ref):
        return cat([ref[b] for b in range(blocks)], 1)

    def begin(ks):
        pr, pi = wide(probe.at[0]), wide(probe.at[1])
        exits = []
        for k in ks:
            wr, wi = wide(win.at[k, 0]), wide(win.at[k, 1])
            exits.append((pr * wr - pi * wi, pr * wi + pi * wr))
        return rows_in(exits, tables)

    def ahead(halves, count):
        for q, value in enumerate(columns_in(halves, tables)):
            freq[q, 0:count * W] = value

    def behind(ks):
        scaled = []
        for q in range(2):
            rows = []
            for i, k in enumerate(ks):
                value = freq[q, i * W:(i + 1) * W]
                fr, fi = value[:, :n], value[:, n:]
                weight = numbers(k)[2]
                factor = weight - (weight * amps[k, :, q * n:(q + 1) * n]) * lax.rsqrt(
                    jnp.maximum(fr * fr + fi * fi, 0.0625))
                rows.append(cat([fr * factor, fi * factor], 1))
            scaled.append(cat(rows, 0))
        for c, value in enumerate(columns_out(*scaled, tables)):
            freq[c, 0:len(ks) * W] = value

    def end(ks, c, first):
        total = None
        for i, (k, (mr, mi)) in enumerate(zip(ks, rows_out(freq[c, 0:len(ks) * W], tables))):
            wr, wi = win[k, 0, c], win[k, 1, c]
            pr, pi = probe[0, c], probe[1, c]
            both = (wr * mr + wi * mi, wr * mi - wi * mr)
            total = both if total is None else [a + b for a, b in zip(total, both)]
            terms[i, 0, c, spare:spare + W] = pr * mr + pi * mi
            terms[i, 1, c, spare:spare + W] = pr * mi - pi * mr
        for ch in range(2):
            grad[c, ch] = total[ch] if first else grad[c, ch] + total[ch]

    def add_terms(ks, first):
        for ch in range(2):
            pieces = [placed(terms.at[i, ch], *numbers(k)[:2]) for i, k in enumerate(ks)]
            for b in range(3):
                piece = sum(p[b] for p in pieces[1:]) + pieces[0][b] if len(ks) > 1 else pieces[0][b]
                acc[b, ch] = piece if first else acc[b, ch] + piece

    def peers(f):
        if G == 2:
            f(1)
        elif G > 2:
            pl.loop(1, G)(f)

    pl.when(not_last)(lambda: scal_side(False).wait_recv())
    pl.when(not_first)(lambda: scal_side(True).wait_recv())
    acc_light[...] = jnp.zeros(acc_light.shape, F32)
    if G <= 2:
        for k in range(G):
            place_light(k)
    else:
        pl.loop(0, G)(place_light)
    acc_light[...] = 1.0 / (acc_light[...] + 0.25 * light_max)
    next_round(0)
    for ch in range(2):
        pl.when(not_last)(lambda: side_bytes(pad.at[2, ch], ch, False).wait_recv())
        pl.when(not_first)(lambda: side_bytes(pad.at[0, ch], ch, True).wait_recv())
    if len(rounds) > 1:
        next_round(1)
    for ch in range(2):
        cut(g, ch)
        peers(lambda j: cut(lax.rem(g + G - j, G), ch))
    look(g, True)
    peers(lambda j: look(lax.rem(g + G - j, G), False))
    chosen = (g, 1 - g) if G == 2 else (g,)
    light_whole[...] = jnp.sum(light_full[...].reshape(blocks * W // 8, 8, B), axis=0)
    pair_copy(light_full.at[1 - p.h, p.rows(p.s)], light_pair.at[0:p.part], 0).start()
    pair_copy(light_whole, light_pair.at[p.part:p.part + 8], 0).start()
    ahead(begin(chosen), len(chosen))
    for i in range(2, len(rounds)):
        next_round(i)
    pair_copy(light_pair, light_pair, 0).wait()
    whole = light_whole[...] + light_pair[p.part:, :]
    for j in range(p.owners):
        light_mine[j, 0:p.chunk] = (light_full[p.h, p.chunk_rows(p.s, j), :]
                                    + light_pair[j * p.chunk:(j + 1) * p.chunk, :])
        light_mine[j, p.chunk:] = whole
    light_red = Reduce(p, light_mine, light_came, light_s)
    light_red.start()

    if G == 2:
        amp_copy(1, True).wait_recv()
    behind(chosen)
    if G > 2:
        for c in range(blocks):
            end(chosen, c, True)
        add_terms(chosen, True)

        def peer_position(j):
            amp_copy(j, True).wait_recv()
            k = lax.rem(g + G - j, G)
            ahead(begin((k,)), 1)
            behind((k,))
            for c in range(blocks):
                end((k,), c, False)
            add_terms((k,), False)

        peers(peer_position)
    else:
        end(chosen, 1 - p.h, True)
    grad_pairs = pair_copy(grad.at[1 - p.h, :, p.rows(p.s)], grad_pair, 1)
    grad_pairs.start()
    if G <= 2:
        end(chosen, p.h, True)
        add_terms(chosen, True)
    grad_pairs.wait()
    for j in range(p.owners):
        grad_mine[j] = (grad[p.h, :, p.chunk_rows(p.s, j), :]
                        + grad_pair[:, j * p.chunk:(j + 1) * p.chunk, :])
    grad_red = Reduce(p, grad_mine, grad_came, grad_s)
    grad_red.start()
    pl.when(not_first)(lambda: edge_copy(False).start())
    pl.when(not_last)(lambda: edge_copy(True).start())

    spread = Gather(p, full, grad_came, sent, line_r, group_r, relay_r)

    @pl.when(p.owner)
    def _():
        light = light_red.total()
        mean = jnp.sum(light[p.chunk:]) * (1.0 / (W * W))
        below = 1.0 / (light[:p.chunk] + 0.25 * mean + 1e-05)
        here = p.chunk_rows(p.s, p.mine)
        total = grad_red.total()
        for ch in range(2):
            full[p.h, p.s, p.mine, ch] = probe[ch, p.h, here, :] - total[ch] * below
        spread.start()

    spread.forward()
    pl.when(not_last)(lambda: edge_copy(False).wait_recv())
    pl.when(not_first)(lambda: edge_copy(True).wait_recv())
    for ch in range(2):
        new_obj[ch] = own[ch] - (acc[1, ch] + edge[0, ch] + edge[1, ch]) * acc_light[...]

    if G > 1:
        bytes_of(pad.at[1, :, 0:(G - 1) * R], own_s.at[0], own_s.at[0]).wait_send()
        bytes_of(amps.at[0:G - 1], amp_s.at[0], amp_s.at[0]).wait_send()
        bytes_of(scal.at[1, 0:G - 1], scal_s.at[0], scal_s.at[1]).wait_send()
    pl.when(not_first)(lambda: side_bytes(pad.at[0], 0, False).wait_send())
    pl.when(not_last)(lambda: side_bytes(pad.at[0], 0, True).wait_send())
    for right, there in ((False, not_first), (True, not_last)):
        pl.when(there)(lambda: scal_side(right).wait_send())
        pl.when(there)(lambda: edge_copy(right).wait_send())
    light_red.finish()
    grad_red.finish()
    spread.finish()
    for ch in range(2):
        for b in range(blocks):
            new_probe[ch, :, b * B:(b + 1) * B] = full[b, :, :, ch].reshape(W, B)
    spread.drain()


def put(obj, probe, obj_out, probe_out, sems):
    copies = [pltpu.make_async_copy(obj, obj_out, sems.at[0]),
              pltpu.make_async_copy(probe, probe_out, sems.at[1])]
    for copy in copies:
        copy.start()
    for copy in copies:
        copy.wait()


def local(T, G, object_field, probe_field, amplitudes, row_start, column_start, live_slots):
    R, B = object_field.shape[1:]
    W = probe_field.shape[1]
    rows = R * G
    p = Plan(T, G, W)
    tables = dft_tables(W)
    spare, blocks = rows - W, W // B
    dma = lambda n: pltpu.SemaphoreType.DMA((max(n, 1),))
    vm = lambda *shape: pltpu.VMEM(shape, F32)

    vmem_limit = 67043328 - 4 * (object_field.size + probe_field.size) - 65536
    smem = pl.BlockSpec(memory_space=pltpu.SMEM)
    hbm = pl.BlockSpec(memory_space=pltpu.HBM)
    vmem = pl.BlockSpec(memory_space=pltpu.VMEM)
    new_obj, new_probe = pl.pallas_call(
        functools.partial(body, T, G),
        out_shape=(pltpu.VMEM(object_field.shape, F32), pltpu.VMEM(probe_field.shape, F32)),
        in_specs=[smem] * 3 + [hbm] * 4,
        out_specs=(vmem, vmem),
        scratch_shapes=[
            pltpu.VMEM((8, 128), jnp.int32),
            pltpu.VMEM((3, G, 8, 128), jnp.int32),
            vm(2, blocks, W, B),
            pltpu.VMEM(tables.shape, BF16),
            dma(4),
            vm(3, 2, rows, B),
            vm(blocks, W, B), vm(G, W, W), vm(G, 2, blocks, W, B),
            vm(2, 2 * W, W), vm(2, 2, blocks, W + 2 * spare, B), vm(blocks, W + 2 * spare, B),
            vm(3, 2, R, B), vm(R, B), vm(2, 2, R, B),
            vm(blocks, W, B), vm(8, B), vm(p.part + 8, B),
            vm(p.owners, p.chunk + 8, B), vm(p.H - 1, p.chunk + 8, B),
            vm(blocks, 2, W, B), vm(2, p.part, B),
            vm(p.owners, 2, p.chunk, B), vm(p.H - 1, 2, p.chunk, B),
            vm(2, p.gs, p.owners, 2, p.chunk, B),
            pltpu.SemaphoreType.REGULAR((max((p.H - 2).bit_length(), 1),)),
            dma(1), dma(4 * G - 4), dma(2), dma(4), dma(1), dma(G - 1), dma(6), dma(2), dma(2),
            dma(2), dma(2), dma(2), dma(2), dma(3), dma(p.owners), dma((p.gs - 1) * p.owners), dma(1),
        ],
        compiler_params=pltpu.CompilerParams(
            collective_id=0, has_side_effects=True, vmem_limit_bytes=vmem_limit),
    )(row_start, column_start, live_slots, object_field, probe_field, amplitudes, tables)
    anywhere = pl.BlockSpec(memory_space=pl.ANY)
    return pl.pallas_call(
        put,
        out_shape=(jax.ShapeDtypeStruct(object_field.shape, F32),
                   jax.ShapeDtypeStruct(probe_field.shape, F32)),
        in_specs=[vmem] * 2,
        out_specs=(anywhere, anywhere),
        scratch_shapes=[dma(2)],
        compiler_params=pltpu.CompilerParams(vmem_limit_bytes=1024 * 1024),
    )(new_obj, new_probe)


def solution(mesh):
    return jax.shard_map(
        functools.partial(local, mesh.shape["tile"], mesh.shape["group"]),
        mesh=mesh,
        in_specs=(
            P(None, "group", "tile"),
            P(),
            P(("tile", "group"), None, None),
            P(("tile", "group")),
            P(("tile", "group")),
            P(("tile", "group")),
        ),
        out_specs=(P(None, "group", "tile"), P()),
        check_vma=False,
    )
```

```python
import functools
import math

import jax
import jax.numpy as jnp
import numpy as np
from jax import lax
from jax.experimental import pallas as pl
from jax.experimental.pallas import tpu as pltpu
from jax.sharding import PartitionSpec as P

MESH = pl.DeviceIdType.MESH
F32 = jnp.float32
BF16 = jnp.bfloat16


def dft_tables(length):
    k = np.arange(length // 2)
    even = (2 * np.outer(k, k)) % length
    odd = np.outer(2 * k + 1, k) % length
    tables = []
    for turns in (even, odd):
        angles = 2.0 * math.pi / length * turns
        cos, sin = np.cos(angles) / math.sqrt(length), np.sin(angles) / math.sqrt(length)
        full = np.block([[cos, sin], [-sin, cos]])
        tables += [full, full.T]
    full = np.stack(tables).astype(np.float32)
    head = full.astype(BF16)
    tail = (full - head.astype(np.float32)).astype(BF16)
    return np.stack([head, tail], axis=1)


EVEN, EVEN_T, ODD, ODD_T = range(4)


def split(x):
    head = x.astype(BF16)
    return head, (x - head.astype(F32)).astype(BF16)


def mm(a, b):
    return jnp.dot(a, b, preferred_element_type=F32)


def cat(parts, axis):
    return jnp.concatenate(parts, axis=axis)


def table_left(table, x):
    head, tail = split(x)
    return mm(cat([table[0], table[0], table[1]], 1), cat([head, tail, head], 0))


def table_right(x, table):
    head, tail = split(x)
    return mm(cat([head, tail, head], 1), cat([table[0], table[0], table[1]], 0))


def rows_in(exits, tables):
    n = exits[0][0].shape[0] // 2
    return [table_left(table, cat([cat([x[:n] + sign * x[n:] for x in parts], 0) for parts in exits], 1))
            for sign, table in ((1, tables[EVEN]), (-1, tables[ODD]))]


def columns_in(halves, tables):
    n = halves[0].shape[0] // 2

    def sides(sign):
        rows = []
        for i in range(halves[0].shape[1] // (2 * n)):
            for y in halves:
                y = y[:, 2 * n * i:2 * n * (i + 1)]
                rows.append(cat([part[:, :n] + sign * part[:, n:] for part in (y[:n], y[n:])], 1))
        return cat(rows, 0)

    return table_right(sides(1), tables[EVEN_T]), table_right(sides(-1), tables[ODD_T])


def columns_out(even, odd, tables):
    e, o = table_right(even, tables[EVEN]), table_right(odd, tables[ODD])
    return e + o, e - o


def rows_out(side, tables):
    n = side.shape[1] // 2
    halves = []
    for q, table in ((0, tables[EVEN_T]), (1, tables[ODD_T])):
        parts = [side[(2 * i + q) * n:(2 * i + q + 1) * n] for i in range(side.shape[0] // (2 * n))]
        halves.append(table_left(table, cat([cat([x[:, :n], x[:, n:]], 0) for x in parts], 1)))
    plus, minus = halves[0] + halves[1], halves[0] - halves[1]
    return [tuple(cat([x[part, n * i:n * (i + 1)] for x in (plus, minus)], 0)
                  for part in (slice(0, n), slice(n, 2 * n))) for i in range(plus.shape[1] // n)]


def remote(src, dst, send, recv, tile, group):
    return pltpu.make_async_remote_copy(
        src_ref=src, dst_ref=dst, send_sem=send, recv_sem=recv,
        device_id={"tile": tile, "group": group}, device_id_type=MESH,
    )


class Plan:
    def __init__(self, T, G, W):
        self.H = T // 2
        self.owners = self.H
        self.first = (self.H - self.owners) // 2
        self.gs = max(n for n in range(1, G + 1) if G % n == 0 and n * self.owners * 8 <= W)
        self.part = W // self.gs
        self.chunk = self.part // self.owners

    def here(self, t, g):
        self.t, self.g = t, g
        self.k, self.h = lax.div(t, 2), lax.rem(t, 2)
        self.partner = t + 1 - 2 * self.h
        self.s = lax.rem(g, self.gs)
        self.mine = self.k - self.first
        self.low = self.k < self.H // 2
        self.owner = jnp.logical_and(self.mine >= 0, self.mine < self.owners)

    def rows(self, s):
        return pl.ds(pl.multiple_of(s * self.part, 8), self.part)

    def chunk_rows(self, s, j):
        return pl.ds(pl.multiple_of(s * self.part + j * self.chunk, 8), self.chunk)

    def far_owner(self, i):
        return lax.rem(i + jnp.where(self.low, self.owners // 2, 0), self.owners)

    def near_owner(self, i):
        return jnp.where(self.low, i, self.owners - 1 - i)

    def far_chip(self, i):
        return jnp.where(self.low, self.H - 1 - i, i)


class Reduce:
    def __init__(self, plan, mine, came, sems):
        self.p, self.mine, self.came, self.sems = plan, mine, came, sems

    def copy(self, j):
        p = self.p
        to = p.first + j
        slot = lax.rem(p.k - to + p.H, p.H) - 1
        return remote(self.mine.at[j], self.came.at[slot], self.sems.at[0], self.sems.at[1],
                      2 * to + p.h, p.g)

    def bytes_of(self, ref):
        return remote(ref, ref, self.sems.at[0], self.sems.at[1], self.p.partner, self.p.g)

    def start(self):
        p = self.p
        for i in range(p.owners):
            j = p.far_owner(i)
            pl.when(p.mine != j)(lambda: self.copy(j).start())

    def total(self):
        self.bytes_of(self.came).wait_recv()
        total = self.mine[self.p.mine]
        for slot in range(self.p.H - 1):
            total = total + self.came[slot]
        return total

    def finish(self):
        p = self.p
        self.bytes_of(self.mine.at[0:p.owners - 1]).wait_send()


class Gather:
    def __init__(self, plan, full, spare, sent, line, group, relay):
        self.p, self.full, self.spare, self.sent = plan, full, spare, sent
        self.line, self.group, self.relay = line, group, relay

    def slot(self, h, s, j):
        return self.full.at[h, s, j]

    def line_copy(self, chip):
        p = self.p
        slot = self.slot(p.h, p.s, p.mine)
        return remote(slot, slot, self.sent.at[0], self.line.at[p.mine], 2 * chip + p.h, p.g)

    def line_arrival(self, j):
        p = self.p
        slot = self.slot(p.h, p.s, j)
        return remote(slot, slot, self.sent.at[0], self.line.at[j], p.partner, p.g)

    def direct_arrival(self, d, j):
        p = self.p
        n = (d - 1) * p.owners + j
        slot = self.slot(p.h, lax.rem(p.s + p.gs - d, p.gs), j)
        return remote(slot, slot, self.sent.at[1], self.group.at[n], p.partner, p.g)

    def relay_copy(self, d, j):
        p = self.p
        slot = self.slot(p.h, lax.rem(p.s + p.gs - d, p.gs), j)
        return remote(slot, slot, self.sent.at[2], self.relay.at[0], p.partner, p.g)

    def bytes_of(self, ref, n):
        return remote(ref, ref, self.sent.at[n], self.relay.at[0], self.p.partner, self.p.g)

    def hand_over(self, j):
        self.relay_copy(0, j).start()

    def direct_copy(self, d, chip):
        p = self.p
        slot = self.slot(p.h, p.s, p.mine)
        return remote(slot, slot, self.sent.at[1], self.group.at[(d - 1) * p.owners + p.mine],
                      2 * chip + p.h, p.g - p.s + lax.rem(p.s + d, p.gs))

    def start(self):
        p = self.p
        self.hand_over(p.mine)
        for i in range(p.H):
            chip = p.far_chip(i)
            for d in range(1, p.gs):
                self.direct_copy(d, chip).start()
            pl.when(p.k != chip)(lambda: self.line_copy(chip).start())

    def forward(self):
        p = self.p
        for i in range(p.owners):
            j = p.near_owner(i)

            @pl.when(p.mine != j)
            def _():
                self.line_arrival(j).wait_recv()
                self.hand_over(j)
        for i in range(p.owners):
            for d in range(1, p.gs):
                j = p.near_owner(i)
                self.direct_arrival(d, j).wait_recv()
                self.relay_copy(d, j).start()

    def finish(self):
        self.bytes_of(self.full.at[1 - self.p.h], 2).wait_recv()

    def drain(self):
        p = self.p
        pl.when(p.owner)(lambda: self.bytes_of(self.spare, 0).wait_send())
        if p.gs > 1:
            self.bytes_of(self.full.at[0, 0:p.gs - 1], 1).wait_send()
        self.bytes_of(self.full.at[0], 2).wait_send()


def body(T, G, row_in, column_in, live_in, obj, probe_in, amp, tables_in, new_obj, new_probe,
         scal_in, scal, probe, tables, load_sem, pad, amp_raw, amps, win, freq, terms, light_terms, acc,
         acc_light, edge, light_full, light_whole, light_pair, light_mine, light_came,
         grad, grad_pair, grad_mine, grad_came, full, reach, own_s, own_r, side_s, side_r, amp_s,
         amp_r, scal_s, edge_s, edge_r, pair_s, pair_r, light_s, grad_s, sent, line_r, group_r,
         relay_r):
    t, g = lax.axis_index("tile"), lax.axis_index("group")
    R, B = obj.shape[1:]
    W = probe.shape[2]
    rows = pad.shape[2]
    spare, blocks = rows - W, W // B
    p = Plan(T, G, W)
    p.here(t, g)
    not_first, not_last = t > 0, t < T - 1

    def span(group):
        return pl.ds(pl.multiple_of(group * R, 8), R)

    own = pad.at[1, :, span(g)]
    loads = [pltpu.make_async_copy(src, dst, load_sem.at[i]) for i, (src, dst) in enumerate(
        [(obj, own), (tables_in, tables)])]
    amp_loads = [pltpu.make_async_copy(amp.at[0, :, b * B:(b + 1) * B], amp_raw.at[b], load_sem.at[3])
                 for b in range(blocks)]
    probe_loads = [pltpu.make_async_copy(probe_in.at[:, :, b * B:(b + 1) * B], probe.at[:, b], load_sem.at[2])
                   for b in range(blocks)]
    for load in amp_loads + probe_loads + loads:
        load.start()

    barrier = pltpu.get_barrier_semaphore()
    count = G - 1
    for j in range(1, G):
        pl.semaphore_signal(barrier, inc=1, device_id={"tile": t, "group": lax.rem(g + j, G)},
                            device_id_type=MESH)
    for d in (-1, 1, -2, 2):
        there = jnp.logical_and(t + d >= 0, t + d < T)

        @pl.when(there)
        def _():
            pl.semaphore_signal(barrier, inc=1, device_id={"tile": t + d, "group": g},
                                device_id_type=MESH)
        count = count + there.astype(jnp.int32)
    line = lax.broadcasted_iota(jnp.int32, scal_in.shape, 0)
    scal_in[...] = jnp.where(line == 0, row_in[0], jnp.where(line == 1, column_in[0], live_in[0]))
    pl.semaphore_wait(barrier, count)

    cut_row = R // 16 * 8
    pieces = [(0, cut_row), (cut_row, R - cut_row)] if cut_row else [(0, R)]

    def piece(group, q):
        return pl.ds(pl.multiple_of(group * R + pieces[q][0], 8), pieces[q][1])

    def to_peer(j, ch, q, arriving):
        peer = lax.rem(g + (G - j if arriving else j), G)
        slot = pad.at[1, ch, piece(peer if arriving else g, q)]
        n = (2 * (j - 1) + ch) * len(pieces) + q
        src = slot if arriving else obj.at[ch, pieces[q][0]:pieces[q][0] + pieces[q][1]]
        return remote(src, slot, own_s.at[0], own_r.at[n], t, peer)

    def to_side(ch, right, src, rows_of):
        dst = pad.at[0 if right else 2, ch, rows_of]
        return remote(src, dst, side_s.at[int(right)], side_r.at[2 * ch + int(right)],
                      t + 1 if right else t - 1, g)

    def side_bytes(ref, ch, right):
        return remote(ref, ref, side_s.at[int(right)], side_r.at[2 * ch + int(right)], p.partner, g)

    def amp_copy(j, arriving):
        peer = lax.rem(g + (G - j if arriving else j), G)
        slot = amps.at[peer if arriving else g]
        return remote(slot, slot, amp_s.at[0], amp_r.at[j - 1], t, peer)

    def scal_copy(j):
        return remote(scal_in, scal.at[1, g], scal_s.at[0], scal_s.at[1], t, lax.rem(g + j, G))

    def scal_side(right):
        return remote(scal.at[1], scal.at[0 if right else 2], scal_s.at[2 + int(right)],
                      scal_s.at[4 + int(right)], t + 1 if right else t - 1, g)

    def bytes_of(ref, send, recv):
        return remote(ref, ref, send, recv, p.partner, g)

    def edge_copy(right):
        return remote(acc.at[2 if right else 0], edge.at[0 if right else 1], edge_s.at[int(right)],
                      edge_r.at[int(right)], t + 1 if right else t - 1, g)

    def pair_copy(src, dst, n):
        return remote(src, dst, pair_s.at[n], pair_r.at[n], p.partner, g)

    def to_sides(ch, src, rows_of):
        pl.when(not_first)(lambda: to_side(ch, False, src, rows_of).start())
        pl.when(not_last)(lambda: to_side(ch, True, src, rows_of).start())

    for j in range(1, G):
        scal_copy(j).start()
    for ch in range(2):
        for q in range(len(pieces)):
            for j in range(1, G):
                to_peer(j, ch, q, False).start()
        to_sides(ch, obj.at[ch], span(g))

    known, rounds = 1, []
    while known < p.H - 1:
        rounds.append(known)
        known *= 2

    def ends(d):
        return [(p.k - d, p.k >= d), (p.k + d, p.k + d < p.H)]

    def tell(i):
        for chip, there in ends(rounds[i]):
            @pl.when(there)
            def _():
                pl.semaphore_signal(reach.at[i], inc=1,
                                    device_id={"tile": 2 * chip + p.h, "group": g}, device_id_type=MESH)

    def hear(i):
        (_, below), (_, above) = ends(rounds[i])
        pl.semaphore_wait(reach.at[i], below.astype(jnp.int32) + above.astype(jnp.int32))

    tell(0)
    scal[1, g] = scal_in[...]

    pltpu.make_async_copy(amp_raw, amp_raw, load_sem.at[3]).wait()
    n = W // 2
    a = cat([cat([amp_raw[b, pl.ds(q, n, stride=2), :] for q in range(2)], 0) for b in range(blocks)], 1)
    at = lax.broadcasted_iota(jnp.int32, (W, W), 1)
    at = jnp.where(at < n, 2 * at, 2 * at - (W - 1))
    order = jnp.where(lax.broadcasted_iota(jnp.int32, (W, W), 0) == at, 1.0, 0.0).astype(BF16)
    top = a.astype(BF16)
    rest = a - top.astype(F32)
    middle, low = split(rest)
    amps[g] = mm(top, order) + (mm(middle, order) + mm(low, order))
    for j in range(1, G):
        amp_copy(j, False).start()

    @pl.when(t == 0)
    def _():
        pad[0] = jnp.zeros(pad.shape[1:], F32)
        edge[0] = jnp.zeros(edge.shape[1:], F32)
        scal[0] = jnp.zeros(scal.shape[1:], jnp.int32)

    @pl.when(t == T - 1)
    def _():
        pad[2] = jnp.zeros(pad.shape[1:], F32)
        edge[1] = jnp.zeros(edge.shape[1:], F32)
        scal[2] = jnp.zeros(scal.shape[1:], jnp.int32)

    terms[:, :, :, 0:spare] = jnp.zeros((2, 2, blocks, spare, B), F32)
    terms[:, :, :, spare + W:] = jnp.zeros((2, 2, blocks, spare, B), F32)
    light_terms[:, 0:spare] = jnp.zeros((blocks, spare, B), F32)
    light_terms[:, spare + W:] = jnp.zeros((blocks, spare, B), F32)

    for load in loads:
        load.wait()
    pltpu.make_async_copy(probe, probe, load_sem.at[2]).wait()
    probe_light = probe[0] * probe[0] + probe[1] * probe[1]
    light_terms[:, spare:spare + W] = probe_light
    light_max = jnp.max(probe_light) + 1e-06

    if G > 1:
        bytes_of(scal.at[1, 0:G - 1], scal_s.at[0], scal_s.at[1]).wait_recv()
    pl.when(not_first)(lambda: scal_side(False).start())
    pl.when(not_last)(lambda: scal_side(True).start())
    for ch in range(2):
        for q in range(len(pieces)):
            for j in range(1, G):
                to_peer(j, ch, q, True).wait_recv()
                rows_of = piece(lax.rem(g + G - j, G), q)
                to_sides(ch, pad.at[1, ch, rows_of], rows_of)

    def next_round(i):
        hear(i)
        if i + 1 < len(rounds):
            tell(i + 1)

    def numbers(k, side=1):
        return scal[side, k, 0, 0], scal[side, k, 1, 0], scal[side, k, 2, 0].astype(F32)

    lane = lax.broadcasted_iota(jnp.int32, (8, B), 1)[0:1]

    def placed(ref, row, column):
        first = g * R + spare - row
        shift = lax.rem(column, B)
        stay = lane >= column
        pieces = [pltpu.roll(ref[b, pl.ds(first, R), :], shift, 1) for b in range(blocks)]
        out = [jnp.where(stay, pieces[0], 0.0)]
        out += [jnp.where(stay, pieces[b], pieces[b - 1]) for b in range(1, blocks)]
        return out + [jnp.where(stay, 0.0, pieces[-1])]

    def cut(k, ch):
        row, column, _ = numbers(k)
        shift = lax.rem(B - lax.rem(column, B), B)
        stay = lane < B - column
        pieces = [pltpu.roll(pad[b, ch, pl.ds(row, W), :], shift, 1) for b in range(blocks + 1)]
        for b in range(blocks):
            win[k, ch, b] = jnp.where(stay, pieces[b], pieces[b + 1])

    def place_light(k):
        total = None
        for side in range(3):
            row, column, weight = numbers(k, side)
            piece = weight * placed(light_terms, row, column)[2 - side]
            total = piece if total is None else total + piece
        acc_light[...] += total

    def look(k, first):
        weight = numbers(k)[2]
        light = weight * (win[k, 0] * win[k, 0] + win[k, 1] * win[k, 1])
        light_full[...] = light if first else light_full[...] + light

    def wide(ref):
        return cat([ref[b] for b in range(blocks)], 1)

    def begin(ks):
        pr, pi = wide(probe.at[0]), wide(probe.at[1])
        exits = []
        for k in ks:
            wr, wi = wide(win.at[k, 0]), wide(win.at[k, 1])
            exits.append((pr * wr - pi * wi, pr * wi + pi * wr))
        return rows_in(exits, tables)

    def ahead(halves, count):
        for q, value in enumerate(columns_in(halves, tables)):
            freq[q, 0:count * W] = value

    def behind(ks):
        scaled = []
        for q in range(2):
            rows = []
            for i, k in enumerate(ks):
                value = freq[q, i * W:(i + 1) * W]
                fr, fi = value[:, :n], value[:, n:]
                weight = numbers(k)[2]
                factor = weight - (weight * amps[k, :, q * n:(q + 1) * n]) * lax.rsqrt(
                    jnp.maximum(fr * fr + fi * fi, 0.0625))
                rows.append(cat([fr * factor, fi * factor], 1))
            scaled.append(cat(rows, 0))
        for c, value in enumerate(columns_out(*scaled, tables)):
            freq[c, 0:len(ks) * W] = value

    def end(ks, c, first):
        total = None
        for i, (k, (mr, mi)) in enumerate(zip(ks, rows_out(freq[c, 0:len(ks) * W], tables))):
            wr, wi = win[k, 0, c], win[k, 1, c]
            pr, pi = probe[0, c], probe[1, c]
            both = (wr * mr + wi * mi, wr * mi - wi * mr)
            total = both if total is None else [a + b for a, b in zip(total, both)]
            terms[i, 0, c, spare:spare + W] = pr * mr + pi * mi
            terms[i, 1, c, spare:spare + W] = pr * mi - pi * mr
        for ch in range(2):
            grad[c, ch] = total[ch] if first else grad[c, ch] + total[ch]

    def add_terms(ks, first):
        for ch in range(2):
            pieces = [placed(terms.at[i, ch], *numbers(k)[:2]) for i, k in enumerate(ks)]
            for b in range(3):
                piece = sum(p[b] for p in pieces[1:]) + pieces[0][b] if len(ks) > 1 else pieces[0][b]
                acc[b, ch] = piece if first else acc[b, ch] + piece

    def peers(f):
        if G == 2:
            f(1)
        elif G > 2:
            pl.loop(1, G)(f)

    pl.when(not_last)(lambda: scal_side(False).wait_recv())
    pl.when(not_first)(lambda: scal_side(True).wait_recv())
    acc_light[...] = jnp.zeros(acc_light.shape, F32)
    if G <= 2:
        for k in range(G):
            place_light(k)
    else:
        pl.loop(0, G)(place_light)
    acc_light[...] = 1.0 / (acc_light[...] + 0.25 * light_max)
    next_round(0)
    for ch in range(2):
        pl.when(not_last)(lambda: side_bytes(pad.at[2, ch], ch, False).wait_recv())
        pl.when(not_first)(lambda: side_bytes(pad.at[0, ch], ch, True).wait_recv())
    if len(rounds) > 1:
        next_round(1)
    for ch in range(2):
        cut(g, ch)
        peers(lambda j: cut(lax.rem(g + G - j, G), ch))
    look(g, True)
    peers(lambda j: look(lax.rem(g + G - j, G), False))
    chosen = (g, 1 - g) if G == 2 else (g,)
    light_whole[...] = jnp.sum(light_full[...].reshape(blocks * W // 8, 8, B), axis=0)
    pair_copy(light_full.at[1 - p.h, p.rows(p.s)], light_pair.at[0:p.part], 0).start()
    pair_copy(light_whole, light_pair.at[p.part:p.part + 8], 0).start()
    ahead(begin(chosen), len(chosen))
    for i in range(2, len(rounds)):
        next_round(i)
    for d in range(1, p.gs):
        pl.semaphore_signal(reach.at[len(rounds)], inc=1, device_id={
            "tile": t, "group": g - p.s + lax.rem(p.s + d, p.gs)}, device_id_type=MESH)
    pair_copy(light_pair, light_pair, 0).wait()
    whole = light_whole[...] + light_pair[p.part:, :]
    for j in range(p.owners):
        light_mine[j, 0:p.chunk] = (light_full[p.h, p.chunk_rows(p.s, j), :]
                                    + light_pair[j * p.chunk:(j + 1) * p.chunk, :])
        light_mine[j, p.chunk:] = whole
    light_red = Reduce(p, light_mine, light_came, light_s)
    light_red.start()

    if G == 2:
        amp_copy(1, True).wait_recv()
    behind(chosen)
    if G > 2:
        for c in range(blocks):
            end(chosen, c, True)
        add_terms(chosen, True)

        def peer_position(j):
            amp_copy(j, True).wait_recv()
            k = lax.rem(g + G - j, G)
            ahead(begin((k,)), 1)
            behind((k,))
            for c in range(blocks):
                end((k,), c, False)
            add_terms((k,), False)

        peers(peer_position)
    else:
        end(chosen, 1 - p.h, True)
    grad_pairs = pair_copy(grad.at[1 - p.h, :, p.rows(p.s)], grad_pair, 1)
    grad_pairs.start()
    if G <= 2:
        end(chosen, p.h, True)
        add_terms(chosen, True)
    grad_pairs.wait()
    for j in range(p.owners):
        grad_mine[j] = (grad[p.h, :, p.chunk_rows(p.s, j), :]
                        + grad_pair[:, j * p.chunk:(j + 1) * p.chunk, :])
    grad_red = Reduce(p, grad_mine, grad_came, grad_s)
    grad_red.start()
    pl.when(not_first)(lambda: edge_copy(False).start())
    pl.when(not_last)(lambda: edge_copy(True).start())

    spread = Gather(p, full, grad_came, sent, line_r, group_r, relay_r)

    if p.gs > 1:
        pl.semaphore_wait(reach.at[len(rounds)], p.gs - 1)

    @pl.when(p.owner)
    def _():
        light = light_red.total()
        mean = jnp.sum(light[p.chunk:]) * (1.0 / (W * W))
        below = 1.0 / (light[:p.chunk] + 0.25 * mean + 1e-05)
        here = p.chunk_rows(p.s, p.mine)
        total = grad_red.total()
        for ch in range(2):
            full[p.h, p.s, p.mine, ch] = probe[ch, p.h, here, :] - total[ch] * below
        spread.start()

    spread.forward()
    pl.when(not_last)(lambda: edge_copy(False).wait_recv())
    pl.when(not_first)(lambda: edge_copy(True).wait_recv())
    for ch in range(2):
        new_obj[ch] = own[ch] - (acc[1, ch] + edge[0, ch] + edge[1, ch]) * acc_light[...]

    if G > 1:
        bytes_of(pad.at[1, :, 0:(G - 1) * R], own_s.at[0], own_s.at[0]).wait_send()
        bytes_of(amps.at[0:G - 1], amp_s.at[0], amp_s.at[0]).wait_send()
        bytes_of(scal.at[1, 0:G - 1], scal_s.at[0], scal_s.at[1]).wait_send()
    pl.when(not_first)(lambda: side_bytes(pad.at[0], 0, False).wait_send())
    pl.when(not_last)(lambda: side_bytes(pad.at[0], 0, True).wait_send())
    for right, there in ((False, not_first), (True, not_last)):
        pl.when(there)(lambda: scal_side(right).wait_send())
        pl.when(there)(lambda: edge_copy(right).wait_send())
    light_red.finish()
    grad_red.finish()
    spread.finish()
    for ch in range(2):
        for b in range(blocks):
            new_probe[ch, :, b * B:(b + 1) * B] = full[b, :, :, ch].reshape(W, B)
    spread.drain()


def put(obj, probe, obj_out, probe_out, sems):
    copies = [pltpu.make_async_copy(obj, obj_out, sems.at[0]),
              pltpu.make_async_copy(probe, probe_out, sems.at[1])]
    for copy in copies:
        copy.start()
    for copy in copies:
        copy.wait()


def local(T, G, object_field, probe_field, amplitudes, row_start, column_start, live_slots):
    R, B = object_field.shape[1:]
    W = probe_field.shape[1]
    rows = R * G
    p = Plan(T, G, W)
    tables = dft_tables(W)
    spare, blocks = rows - W, W // B
    dma = lambda n: pltpu.SemaphoreType.DMA((max(n, 1),))
    vm = lambda *shape: pltpu.VMEM(shape, F32)

    vmem_limit = 67043328 - 4 * (object_field.size + probe_field.size) - 65536
    smem = pl.BlockSpec(memory_space=pltpu.SMEM)
    hbm = pl.BlockSpec(memory_space=pltpu.HBM)
    vmem = pl.BlockSpec(memory_space=pltpu.VMEM)
    new_obj, new_probe = pl.pallas_call(
        functools.partial(body, T, G),
        out_shape=(pltpu.VMEM(object_field.shape, F32), pltpu.VMEM(probe_field.shape, F32)),
        in_specs=[smem] * 3 + [hbm] * 4,
        out_specs=(vmem, vmem),
        scratch_shapes=[
            pltpu.VMEM((8, 128), jnp.int32),
            pltpu.VMEM((3, G, 8, 128), jnp.int32),
            vm(2, blocks, W, B),
            pltpu.VMEM(tables.shape, BF16),
            dma(4),
            vm(3, 2, rows, B),
            vm(blocks, W, B), vm(G, W, W), vm(G, 2, blocks, W, B),
            vm(2, 2 * W, W), vm(2, 2, blocks, W + 2 * spare, B), vm(blocks, W + 2 * spare, B),
            vm(3, 2, R, B), vm(R, B), vm(2, 2, R, B),
            vm(blocks, W, B), vm(8, B), vm(p.part + 8, B),
            vm(p.owners, p.chunk + 8, B), vm(p.H - 1, p.chunk + 8, B),
            vm(blocks, 2, W, B), vm(2, p.part, B),
            vm(p.owners, 2, p.chunk, B), vm(p.H - 1, 2, p.chunk, B),
            vm(2, p.gs, p.owners, 2, p.chunk, B),
            pltpu.SemaphoreType.REGULAR(((p.H - 2).bit_length() + 1,)),
            dma(1), dma(4 * G - 4), dma(2), dma(4), dma(1), dma(G - 1), dma(6), dma(2), dma(2),
            dma(2), dma(2), dma(2), dma(2), dma(3), dma(p.owners), dma((p.gs - 1) * p.owners), dma(1),
        ],
        compiler_params=pltpu.CompilerParams(
            collective_id=0, has_side_effects=True, vmem_limit_bytes=vmem_limit),
    )(row_start, column_start, live_slots, object_field, probe_field, amplitudes, tables)
    anywhere = pl.BlockSpec(memory_space=pl.ANY)
    return pl.pallas_call(
        put,
        out_shape=(jax.ShapeDtypeStruct(object_field.shape, F32),
                   jax.ShapeDtypeStruct(probe_field.shape, F32)),
        in_specs=[vmem] * 2,
        out_specs=(anywhere, anywhere),
        scratch_shapes=[dma(2)],
        compiler_params=pltpu.CompilerParams(vmem_limit_bytes=1024 * 1024),
    )(new_obj, new_probe)


def solution(mesh):
    return jax.shard_map(
        functools.partial(local, mesh.shape["tile"], mesh.shape["group"]),
        mesh=mesh,
        in_specs=(
            P(None, "group", "tile"),
            P(),
            P(("tile", "group"), None, None),
            P(("tile", "group")),
            P(("tile", "group")),
            P(("tile", "group")),
        ),
        out_specs=(P(None, "group", "tile"), P()),
        check_vma=False,
    )
```
